512 devices in a mesh: slab: 128 (over y, z, core), case: 4 (over x).
Axes of the slice: x: 4, y: 8, z: 8, core: 2. Of those that a mesh axis runs over, the one named last changes fastest.
Arguments:
- pressure: float32 [64, 512], replicated, may hold values from -9 to 9
- panel: int32 [1536, 4, 128], P('slab'), may hold values from 0 to 511
- flags: int32 [1536, 4, 128], P('slab'), may hold values 0 or 1
- diagonal: float32 [1536, 4, 128], P('slab'), may hold values from 0.25 to 4
Outputs:
- fields: float32 [64, 1536, 4, 128], P('case', 'slab')
- gram: float32 [64, 64], P('case')
- cross: float32 [64, 64], P('case')
The draws below stay inside these ranges and needn't reach their ends.
All inputs are finite; a program needn't handle non-finite values. No bound on the sum of `flags` on one device may be relied on, other than what follows from the above.
Results may differ from the reference program's by a relative error of at most 0.00005.
Values sent between devices are 32-bit elements; how exact they have to be, the bound alone decides.
A program may use at most 64 MiB of HBM per device.

```python
import math
import jax
import jax.numpy as jnp
from jax import lax

NR = 4
NC = 128
NCASE = 64
PANELS = 512
NA = 1536


def draw_pressure(key, part):
    first_key, second_key, third_key = jax.random.split(key, 3)
    amplitude = jax.random.uniform(first_key, (NCASE, 1), jnp.float32, 0.5, 1.5)
    pattern = jnp.clip(jax.random.normal(second_key, (1, PANELS), jnp.float32), -4.0, 4.0)
    variation = 0.7 * jnp.clip(jax.random.normal(third_key, (NCASE, PANELS), jnp.float32), -4.0, 4.0)
    return amplitude * pattern + variation


def place_ends(entries, rng, least, largest):
    longest = entries.shape.index(max(entries.shape))
    spots = []
    for shift in (0, 1):
        where = [jax.random.randint(jax.random.fold_in(rng, axis), (), 0, length) for axis, length in enumerate(entries.shape)]
        where[longest] = (where[longest] + shift) % entries.shape[longest]
        spots.append(tuple(where))
    return entries.at[spots[0]].set(least).at[spots[1]].set(largest)


def levels(own_key, extent, pieces, low, high):
    loudness, own = 1.0, jax.random.fold_in(own_key, 6)
    for position, blocks in pieces:
        draws = jnp.exp(jax.random.uniform(jax.random.fold_in(own, position), (blocks,), jnp.float32, low / len(pieces), high / len(pieces)))
        loudness = loudness * jnp.repeat(draws, extent[position] // blocks).reshape([-1 if axis == position else 1 for axis in range(len(extent))])
    return loudness


def setup_inputs(seed: int = 0) -> dict:
    key_of = jax.random.split(jax.random.key(seed), 5)
    return {
        "pressure": draw_pressure(jax.random.fold_in(key_of[4], 71), 0),
        "panel": place_ends(jax.random.randint(key_of[1], (NA, NR, NC), 0, PANELS), jax.random.fold_in(key_of[1], 1), 0, PANELS - 1).astype(jnp.int32),
        "flags": place_ends((jax.random.randint(key_of[2], (NA, NR, NC), 0, 8) < 1).astype(jnp.int32), jax.random.fold_in(key_of[2], 1), 0, 1),
        "diagonal": jnp.clip(jnp.exp(math.log(4.0) - 2.7725887 * jax.random.uniform(key_of[3], (NA, NR, NC), jnp.float32) ** levels(key_of[3], (NA, NR, NC), ((0, 128),), -0.2, 0.2)), 0.25, 4.0),
    }


damping = 0.7
penalty = 4.0
highest = lax.Precision.HIGHEST


def transverse(field):
    beside_all = jnp.roll(field, 1, axis=-1) + jnp.roll(field, -1, axis=-1)
    zero_row = jnp.zeros_like(field[..., :1, :])
    inward = jnp.concatenate([zero_row, field[..., :-1, :]], axis=-2)
    outward = jnp.concatenate([field[..., 1:, :], zero_row], axis=-2)
    return beside_all + inward + outward


def stencil(field, below, above, coeff, weight):
    return (coeff + 2.0 * weight + 4.0) * field - weight * (below + above) - transverse(field)


def apply_local(field, coeff, weight):
    zero_layer = jnp.zeros_like(field[:, :1])
    below = jnp.concatenate([zero_layer, field[:, :-1]], axis=1)
    above = jnp.concatenate([field[:, 1:], zero_layer], axis=1)
    return stencil(field, below, above, coeff, weight)


def smooth_local(field, rhs, coeff, weight):
    return field + damping * (rhs - apply_local(field, coeff, weight)) / (coeff + 2.0 * weight + 4.0)


def restrict(fine):
    even = fine[:, 0::2]
    odd = fine[:, 1::2]
    odd_before = jnp.concatenate([jnp.zeros_like(odd[:, :1]), odd[:, :-1]], axis=1)
    return 0.5 * even + 0.25 * (odd + odd_before)


def prolong(coarse):
    following = jnp.concatenate([coarse[:, 1:], jnp.zeros_like(coarse[:, :1])], axis=1)
    middle = 0.5 * (coarse + following)
    stacked = jnp.stack([coarse, middle], axis=2)
    shape = coarse.shape
    return stacked.reshape(shape[0], 2 * shape[1], shape[2], shape[3])


def vcycle(rhs, coeff, level):
    weight = 0.25 ** level
    field = damping * rhs / (coeff + 2.0 * weight + 4.0)
    if level == 2:
        for sweep in range(3):
            field = smooth_local(field, rhs, coeff, weight)
        return field
    field = smooth_local(field, rhs, coeff, weight)
    leftover = rhs - apply_local(field, coeff, weight)
    coarse_coeff = 0.5 * (coeff[0::2] + coeff[1::2])
    field = field + prolong(vcycle(restrict(leftover), coarse_coeff, level + 1))
    for sweep in range(2):
        field = smooth_local(field, rhs, coeff, weight)
    return field


def reference(pressure, panel, flags, diagonal):
    coeff = diagonal + penalty * flags.astype(jnp.float32)
    keep = 1.0 - flags.astype(jnp.float32)
    positions = jnp.arange(NA).astype(jnp.float32)
    span = (1.0 + 2.0 * positions / NA)[:, None, None]

    def one_case(load_row):
        rhs = jnp.take(load_row, panel.astype(jnp.int32), axis=0) * span * keep
        rhs = rhs[None]
        field = vcycle(rhs, coeff, 0)
        image = apply_local(field, coeff, 1.0)
        return field[0], image[0], rhs[0]

    fields, images, loads = lax.map(one_case, pressure)
    scale = 1.0 / (NA * NR * NC)
    fields_flat = fields.reshape(NCASE, -1)
    gram = jnp.dot(images.reshape(NCASE, -1), fields_flat.T, precision=highest, preferred_element_type=jnp.float32) * scale
    cross = jnp.dot(loads.reshape(NCASE, -1), fields_flat.T, precision=highest, preferred_element_type=jnp.float32) * scale
    return (fields, gram, cross)
```

```python
import functools

import jax
import jax.numpy as jnp
from jax import lax
from jax.experimental import pallas as pl
from jax.experimental.pallas import tpu as pltpu
from jax.sharding import PartitionSpec as P

MESH = pl.DeviceIdType.MESH
ZSIZE = 8
YSIZE = 8
CORES = 2
CASES = 4
REACH = 3
BASE = 29
highest = lax.Precision.HIGHEST


def halo_kernel(slabs, panel, flags, diagonal, panel_out, flags_out, diagonal_out, send, recv, own):
    slab = lax.axis_index("slab")
    barrier = pltpu.get_barrier_semaphore()
    shifts = [d for d in range(-REACH, REACH + 1) if d != 0]
    for d in shifts:
        there = lax.rem(slab + d + slabs, slabs)
        pl.semaphore_signal(barrier, inc=1, device_id={"slab": there}, device_id_type=MESH)
    locals_ = []
    for n, (src, dst) in enumerate(((panel, panel_out), (flags, flags_out), (diagonal, diagonal_out))):
        copy = pltpu.make_async_copy(src, dst.at[REACH], own.at[n])
        copy.start()
        locals_.append(copy)
    pl.semaphore_wait(barrier, len(shifts))
    copies = []
    layers = panel.shape[0]
    for d in sorted(shifts, key=lambda d: -abs(d)):
        there = lax.rem(slab + d + slabs, slabs)
        slot = REACH - d
        start, count = {3: (layers - 5, 5), -3: (0, 6)}.get(d, (0, layers))
        for n, (src, dst) in enumerate(((panel, panel_out), (flags, flags_out), (diagonal, diagonal_out))):
            copy = pltpu.make_async_remote_copy(
                src_ref=src.at[pl.ds(start, count)],
                dst_ref=dst.at[slot, pl.ds(start, count)],
                send_sem=send.at[n, slot],
                recv_sem=recv.at[n, slot],
                device_id={"slab": there},
                device_id_type=MESH,
            )
            copy.start()
            copies.append(copy)
    for copy in locals_:
        copy.wait()
    for copy in copies:
        copy.wait()


def exchange_halo(panel, flags, diagonal, slabs):
    shape = (2 * REACH + 1,) + panel.shape
    anyspace = pl.BlockSpec(memory_space=pl.ANY)
    return pl.pallas_call(
        functools.partial(halo_kernel, slabs),
        out_shape=[
            jax.ShapeDtypeStruct(shape, jnp.int32),
            jax.ShapeDtypeStruct(shape, jnp.int32),
            jax.ShapeDtypeStruct(shape, jnp.float32),
        ],
        in_specs=[anyspace] * 3,
        out_specs=[anyspace] * 3,
        scratch_shapes=[
            pltpu.SemaphoreType.DMA((3, 2 * REACH + 1)),
            pltpu.SemaphoreType.DMA((3, 2 * REACH + 1)),
            pltpu.SemaphoreType.DMA((3,)),
        ],
        compiler_params=pltpu.CompilerParams(collective_id=1, has_side_effects=True),
        name="halo",
    )(panel, flags, diagonal)


def lateral(v):
    flat = v.reshape(-1, v.shape[-1])
    sides = pltpu.roll(flat, 1, 1) + pltpu.roll(flat, flat.shape[1] - 1, 1)
    edge = jnp.zeros_like(v[:1])
    inward = jnp.concatenate([edge, v[:-1]], axis=0)
    outward = jnp.concatenate([v[1:], edge], axis=0)
    return sides.reshape(v.shape) + (inward + outward)


def spread(row):
    return jnp.broadcast_to(row[:, None, None, :], (row.shape[0], 1, 8, row.shape[1]))


def lookup(blocks, panel_row):
    out = []
    for r in range(panel_row.shape[0]):
        where = jnp.broadcast_to(panel_row[r : r + 1], (8, panel_row.shape[1]))
        low = where & 127
        high = where >> 7
        halves = []
        for pieces in blocks:
            found = jnp.take_along_axis(pieces[0], low, axis=1)
            for j in range(1, len(pieces)):
                found = jnp.where(high == j, jnp.take_along_axis(pieces[j], low, axis=1), found)
            halves.append(found)
        out.append(jnp.stack(halves))
    return jnp.stack(out)


def vcycle_kernel(total, pressure, panel, flags, diagonal, fields, ext, loads, chunk_diag,
                  b0, c0, v0a, v0b, r0, w0, d0, b1, c1, v1a, v1b, r1, w1, d1, b2, v2a, v2b, w2):
    slab = lax.axis_index("slab")
    group = lax.axis_index("case")
    own = fields.shape[1]
    pad = REACH * own
    cases = fields.shape[0]
    first = pl.multiple_of(group * cases, cases)
    blocks = [
        [pressure[pl.ds(first + 8 * h, 8), 128 * j : 128 * j + 128] for j in range(pressure.shape[1] // 128)]
        for h in range(cases // 8)
    ]

    def inside(p, level):
        g = p + slab * (own >> level)
        return (g >= pad >> level) & (g < (total + pad) >> level)

    def span_of(p):
        at = (p + slab * own - pad).astype(jnp.float32)
        return 1.0 + 2.0 * at / total

    def setup(i, _):
        p = i + (pad - BASE)
        held = flags[p].astype(jnp.float32)
        coeff = diagonal[p] + 4.0 * held
        c0[i] = coeff
        full = coeff + 6.0
        within = inside(p, 0)
        w = spread(jnp.where(within, 0.7 / full, 0.0))
        factor = spread(jnp.where(within, (1.0 - held) * span_of(p), 0.0))
        w0[i] = w
        d0[i] = spread(full)
        rhs = lookup(blocks, panel[p]) * factor
        b0[i] = rhs
        v0a[i] = w * rhs
        return 0

    lax.fori_loop(0, 71, setup, 0)

    def sweep(src, dst, rhs, w, weight, base, low, high):
        def body(i, _):
            v = src[i]
            near = src[i - 1] + src[i + 1]
            if weight != 1.0:
                near = weight * near
            dst[i] = 0.3 * v + w[i] * (rhs[i] + near + lateral(v))
            return 0

        lax.fori_loop(low + base, high + base, body, 0)

    def residual(src, dst, rhs, full, weight, base, low, high, level):
        def body(i, _):
            v = src[i]
            near = src[i - 1] + src[i + 1]
            if weight != 1.0:
                near = weight * near
            left = rhs[i] - full[i] * v + (near + lateral(v))
            dst[i] = jnp.where(inside(i + ((pad >> level) - base), level), left, 0.0)
            return 0

        lax.fori_loop(low + base, high + base, body, 0)

    def restrict(fine, fine_base, cfine, rhs, ccoarse, w, full, vinit, weight, base, low, high, level):
        def body(k, _):
            at = 2 * k + (fine_base + 2 * low)
            i = k + (low + base)
            value = 0.5 * fine[at] + 0.25 * (fine[at + 1] + fine[at - 1])
            coeff = 0.5 * (cfine[at] + cfine[at + 1])
            diag = coeff + (2.0 * weight + 4.0)
            if ccoarse is not None:
                ccoarse[i] = coeff
                full[i] = spread(diag)
            scale = spread(jnp.where(inside(k + (low + (pad >> level)), level), 0.7 / diag, 0.0))
            w[i] = scale
            rhs[i] = value
            vinit[i] = scale * value
            return 0

        lax.fori_loop(0, high - low, body, 0)

    def prolong(coarse, coarse_base, v, base, low, high, level):
        def body(k, _):
            here = coarse[k + (low + coarse_base)]
            after = coarse[k + (low + coarse_base + 1)]
            at = 2 * k + (2 * low + base)
            p = 2 * k + (2 * low + (pad >> level))
            v[at] = v[at] + jnp.where(inside(p, level), here, 0.0)
            v[at + 1] = v[at + 1] + jnp.where(inside(p + 1, level), 0.5 * (here + after), 0.0)
            return 0

        lax.fori_loop(0, high - low, body, 0)

    sweep(v0a, v0b, b0, w0, 1.0, BASE, -28, 41)
    residual(v0b, r0, b0, d0, 1.0, BASE, -27, 40, 0)
    restrict(r0, BASE, c0, b1, c1, w1, d1, v1a, 0.25, 14, -13, 20, 1)
    sweep(v1a, v1b, b1, w1, 0.25, 14, -12, 19)
    residual(v1b, r1, b1, d1, 0.25, 14, -11, 18, 1)
    restrict(r1, 14, c1, b2, None, w2, None, v2a, 0.0625, 6, -5, 9, 2)
    sweep(v2a, v2b, b2, w2, 0.0625, 6, -4, 8)
    sweep(v2b, v2a, b2, w2, 0.0625, 6, -3, 7)
    sweep(v2a, v2b, b2, w2, 0.0625, 6, -2, 6)
    prolong(v2b, 6, v1b, 14, -2, 5, 1)
    sweep(v1b, v1a, b1, w1, 0.25, 14, -3, 9)
    sweep(v1a, v1b, b1, w1, 0.25, 14, -2, 8)
    prolong(v1b, 14, v0b, BASE, -2, 7, 0)
    even = v1b[7 + 14]
    v0b[14 + BASE] = v0b[14 + BASE] + jnp.where(inside(14 + pad, 0), even, 0.0)
    sweep(v0b, v0a, b0, w0, 1.0, BASE, -2, 14)

    def last(k, _):
        i = k + (BASE - 1)
        v = v0a[i]
        near = v0a[i - 1] + v0a[i + 1]
        ext[k] = 0.3 * v + w0[i] * (b0[i] + near + lateral(v))
        return 0

    lax.fori_loop(0, own + 2, last, 0)
    for f in range(own):
        for r in range(fields.shape[2]):
            fields[:, f, r, :] = ext[f + 1, r].reshape(cases, 128)

    share = own // CASES
    for j in range(share):
        p = group * share + (pad + j)
        held = flags[p].astype(jnp.float32)
        factor = spread((1.0 - held) * span_of(p))
        chunk_diag[j] = spread(diagonal[p] + 4.0 * held + 6.0)
        every = [
            [pressure[8 * h : 8 * h + 8, 128 * k : 128 * k + 128] for k in range(pressure.shape[1] // 128)]
            for h in range(pressure.shape[0] // 8)
        ]
        loads[j] = lookup(every, panel[p]) * factor


def solve(pressure, panel, flags, diagonal, total, own, radial, around, cases):
    halves = cases // 8
    vm = pl.BlockSpec(memory_space=pltpu.VMEM)
    share = own // CASES
    ext_shape = (own + 2, radial, halves, 8, around)

    def field(n):
        return pltpu.VMEM((n, radial, halves, 8, around), jnp.float32)

    def wide(n):
        return pltpu.VMEM((n, radial, 1, 8, around), jnp.float32)

    def plain(n):
        return pltpu.VMEM((n, radial, around), jnp.float32)

    return pl.pallas_call(
        functools.partial(vcycle_kernel, total),
        out_shape=[
            jax.ShapeDtypeStruct((cases, own, radial, around), jnp.float32),
            jax.ShapeDtypeStruct(ext_shape, jnp.float32),
            jax.ShapeDtypeStruct((share, radial, pressure.shape[0] // 8, 8, around), jnp.float32),
            jax.ShapeDtypeStruct((share, radial, 1, 8, around), jnp.float32),
        ],
        in_specs=[vm] * 4,
        out_specs=[vm] * 4,
        scratch_shapes=[
            field(72), plain(72), field(72), field(72), field(72), wide(72), wide(72),
            field(36), plain(36), field(36), field(36), field(36), wide(36), wide(36),
            field(16), field(16), field(16), wide(16),
        ],
        compiler_params=pltpu.CompilerParams(vmem_limit_bytes=48 * 1024 * 1024),
        name="vcycle",
    )(pressure, panel, flags, diagonal)


def gram_kernel(ext, loads, chunk_diag, out, pieces, rows, along_z, along_y,
                piece_send, piece_recv, row_send, row_recv, z_send, z_recv, y_send, y_recv, own_sem):
    slab = lax.axis_index("slab")
    group = lax.axis_index("case")
    core = lax.rem(slab, CORES)
    z = lax.rem(slab // CORES, ZSIZE)
    y = slab // (CORES * ZSIZE)
    pair = slab - core
    share = loads.shape[0]
    barrier = pltpu.get_barrier_semaphore()

    mates = [(dx, dc) for dc in range(CORES) for dx in range(CASES) if (dx, dc) != (0, 0)]

    def mate(dx, dc):
        return (pair + lax.rem(core + dc, CORES), lax.rem(group + dx, CASES))

    def z_mate(d):
        return (y * (ZSIZE * CORES) + lax.rem(z + d, ZSIZE) * CORES + core, group)

    def y_mate(d):
        return (lax.rem(y + d, YSIZE) * (ZSIZE * CORES) + z * CORES + core, group)

    everyone = [mate(dx, dc) for dx, dc in mates]
    everyone += [z_mate(d) for d in range(1, ZSIZE)]
    everyone += [y_mate(d) for d in range(1, YSIZE)]
    for device in everyone:
        pl.semaphore_signal(barrier, inc=1, device_id=device, device_id_type=MESH)
    keep = pltpu.make_async_copy(ext.at[pl.ds(group * share, share + 2)], pieces.at[group], own_sem)
    keep.start()
    pl.semaphore_wait(barrier, len(everyone))

    copies = []
    for dx in (2, 1, 3):
        there = lax.rem(group + dx, CASES)
        copy = pltpu.make_async_remote_copy(
            src_ref=ext.at[pl.ds(there * share, share + 2)],
            dst_ref=pieces.at[group],
            send_sem=piece_send.at[there],
            recv_sem=piece_recv.at[group],
            device_id=(slab, there),
            device_id_type=MESH,
        )
        copy.start()
        copies.append(copy)
    keep.wait()
    for dx in (1, 2, 3):
        source = lax.rem(group + dx, CASES)
        pltpu.make_async_remote_copy(
            src_ref=pieces.at[source],
            dst_ref=pieces.at[source],
            send_sem=piece_send.at[source],
            recv_sem=piece_recv.at[source],
            device_id=(slab, source),
            device_id_type=MESH,
        ).wait_recv()

    radial, around = ext.shape[1], ext.shape[-1]
    image_parts, field_parts, load_parts = [], [], []
    for j in range(share):
        by_slot_image, by_slot_field = [], []
        for g in range(CASES):
            v = pieces[g, j + 1]
            near = pieces[g, j] + pieces[g, j + 2]
            by_slot_image.append(chunk_diag[j] * v - near - lateral(v))
            by_slot_field.append(v)
        for r in range(radial):
            image_parts.append(jnp.concatenate([v[r].reshape(-1, around) for v in by_slot_image], axis=0))
            field_parts.append(jnp.concatenate([v[r].reshape(-1, around) for v in by_slot_field], axis=0))
            load_parts.append(loads[j, r].reshape(-1, around))
    left = jnp.concatenate(
        [jnp.concatenate(image_parts, axis=1), jnp.concatenate(load_parts, axis=1)], axis=0
    )
    right = jnp.concatenate(field_parts, axis=1)
    product = lax.dot_general(
        left, right, (((1,), (1,)), ((), ())), precision=highest, preferred_element_type=jnp.float32
    )
    count = right.shape[0]
    both = jnp.concatenate([product[:count], product[count:]], axis=1)
    per = count // CASES
    me = group * CORES + core
    outgoing = rows.at[0]
    for g in range(CASES):
        rows[0, g] = both[g * per : (g + 1) * per]
    for dx, dc in mates:
        there_slab, there_group = mate(dx, dc)
        copy = pltpu.make_async_remote_copy(
            src_ref=rows.at[0, there_group],
            dst_ref=rows.at[1 + core, group],
            send_sem=row_send.at[dx, dc],
            recv_sem=row_recv.at[core, group],
            device_id=(there_slab, there_group),
            device_id_type=MESH,
        )
        copy.start()
        copies.append(copy)
    rows[1 + core, group] = rows[0, group]
    for dx, dc in mates:
        source_core, source_group = lax.rem(core + dc, CORES), lax.rem(group + dx, CASES)
        pltpu.make_async_remote_copy(
            src_ref=rows.at[1 + source_core, source_group],
            dst_ref=rows.at[1 + source_core, source_group],
            send_sem=row_send.at[dx, dc],
            recv_sem=row_recv.at[source_core, source_group],
            device_id=(slab, group),
            device_id_type=MESH,
        ).wait_recv()
    total = rows[1, 0]
    for c in range(CORES):
        for g in range(CASES):
            if (c, g) != (0, 0):
                total = total + rows[1 + c, g]

    def combine(total, slots, at, size, device, send, recv):
        slots[at] = total
        for d in range(1, size):
            copy = pltpu.make_async_remote_copy(
                src_ref=slots.at[at],
                dst_ref=slots.at[at],
                send_sem=send.at[d],
                recv_sem=recv.at[at],
                device_id=device(d),
                device_id_type=MESH,
            )
            copy.start()
            copies.append(copy)
        for d in range(1, size):
            source = lax.rem(at + d, size)
            pltpu.make_async_remote_copy(
                src_ref=slots.at[source],
                dst_ref=slots.at[source],
                send_sem=send.at[d],
                recv_sem=recv.at[source],
                device_id=device(d),
                device_id_type=MESH,
            ).wait_recv()
        result = slots[0]
        for d in range(1, size):
            result = result + slots[d]
        return result

    total = combine(total, along_z, z, ZSIZE, z_mate, z_send, z_recv)
    total = combine(total, along_y, y, YSIZE, y_mate, y_send, y_recv)
    out[...] = total
    for copy in copies:
        copy.wait_send()


def reduce_gram(ext, loads, chunk_diag, per):
    vm = pl.BlockSpec(memory_space=pltpu.VMEM)
    share = loads.shape[0]
    width = 2 * per * CASES
    return pl.pallas_call(
        gram_kernel,
        out_shape=jax.ShapeDtypeStruct((per, width), jnp.float32),
        in_specs=[vm] * 3,
        out_specs=vm,
        scratch_shapes=[
            pltpu.VMEM((CASES, share + 2) + ext.shape[1:], jnp.float32),
            pltpu.VMEM((1 + CORES, CASES, per, width), jnp.float32),
            pltpu.VMEM((ZSIZE, per, width), jnp.float32),
            pltpu.VMEM((YSIZE, per, width), jnp.float32),
            pltpu.SemaphoreType.DMA((CASES,)),
            pltpu.SemaphoreType.DMA((CASES,)),
            pltpu.SemaphoreType.DMA((CASES, CORES)),
            pltpu.SemaphoreType.DMA((CORES, CASES)),
            pltpu.SemaphoreType.DMA((ZSIZE,)),
            pltpu.SemaphoreType.DMA((ZSIZE,)),
            pltpu.SemaphoreType.DMA((YSIZE,)),
            pltpu.SemaphoreType.DMA((YSIZE,)),
            pltpu.SemaphoreType.DMA,
        ],
        compiler_params=pltpu.CompilerParams(collective_id=2, has_side_effects=True),
        name="gram",
    )(ext, loads, chunk_diag)


def local(pressure, panel, flags, diagonal):
    layers, radial, around = panel.shape
    slabs = lax.axis_size("slab")
    groups = lax.axis_size("case")
    per = pressure.shape[0] // groups
    total = layers * slabs
    spreads = exchange_halo(panel, flags, diagonal, slabs)
    wide = [x.reshape((-1,) + panel.shape[1:]) for x in spreads]
    fields, ext, loads, chunk_diag = solve(pressure, *wide, total, layers, radial, around, per)
    sums = reduce_gram(ext, loads, chunk_diag, per)
    scale = 1.0 / (total * radial * around)
    sums = sums * scale
    count = pressure.shape[0]
    return (fields, sums[:, :count], sums[:, count:])


def solution(mesh):
    in_specs = (P(), P("slab", None, None), P("slab", None, None), P("slab", None, None))
    out_specs = (P("case", "slab", None, None), P("case", None), P("case", None))
    return jax.shard_map(local, mesh=mesh, in_specs=in_specs, out_specs=out_specs, check_vma=False)
```

```python
import functools

import jax
import jax.numpy as jnp
from jax import lax
from jax.experimental import pallas as pl
from jax.experimental.pallas import tpu as pltpu
from jax.sharding import PartitionSpec as P

MESH = pl.DeviceIdType.MESH
ZSIZE = 8
YSIZE = 8
CORES = 2
CASES = 4
REACH = 3
BASE = 29
SETUP_STEP = 18
SWEEP_STEP = 36
COARSE_STEP = 11
highest = lax.Precision.HIGHEST


def halo_kernel(slabs, panel, flags, diagonal, panel_out, flags_out, diagonal_out, send, recv, own):
    slab = lax.axis_index("slab")
    barrier = pltpu.get_barrier_semaphore()
    shifts = [d for d in range(-REACH, REACH + 1) if d != 0]
    for d in shifts:
        there = lax.rem(slab + d + slabs, slabs)
        pl.semaphore_signal(barrier, inc=1, device_id={"slab": there}, device_id_type=MESH)
    locals_ = []
    for n, (src, dst) in enumerate(((panel, panel_out), (flags, flags_out), (diagonal, diagonal_out))):
        copy = pltpu.make_async_copy(src, dst.at[REACH], own.at[n])
        copy.start()
        locals_.append(copy)
    pl.semaphore_wait(barrier, len(shifts))
    copies = []
    layers = panel.shape[0]
    for d in sorted(shifts, key=lambda d: -abs(d)):
        there = lax.rem(slab + d + slabs, slabs)
        slot = REACH - d
        start, count = {3: (layers - 5, 5), -3: (0, 6)}.get(d, (0, layers))
        for n, (src, dst) in enumerate(((panel, panel_out), (flags, flags_out), (diagonal, diagonal_out))):
            copy = pltpu.make_async_remote_copy(
                src_ref=src.at[pl.ds(start, count)],
                dst_ref=dst.at[slot, pl.ds(start, count)],
                send_sem=send.at[n, slot],
                recv_sem=recv.at[n, slot],
                device_id={"slab": there},
                device_id_type=MESH,
            )
            copy.start()
            copies.append(copy)
    for copy in locals_:
        copy.wait()
    for copy in copies:
        copy.wait()


def exchange_halo(panel, flags, diagonal, slabs):
    shape = (2 * REACH + 1,) + panel.shape
    anyspace = pl.BlockSpec(memory_space=pl.ANY)
    return pl.pallas_call(
        functools.partial(halo_kernel, slabs),
        out_shape=[
            jax.ShapeDtypeStruct(shape, jnp.int32),
            jax.ShapeDtypeStruct(shape, jnp.int32),
            jax.ShapeDtypeStruct(shape, jnp.float32),
        ],
        in_specs=[anyspace] * 3,
        out_specs=[anyspace] * 3,
        scratch_shapes=[
            pltpu.SemaphoreType.DMA((3, 2 * REACH + 1)),
            pltpu.SemaphoreType.DMA((3, 2 * REACH + 1)),
            pltpu.SemaphoreType.DMA((3,)),
        ],
        compiler_params=pltpu.CompilerParams(collective_id=1, has_side_effects=True),
        name="halo",
    )(panel, flags, diagonal)


def lateral(v):
    flat = v.reshape(-1, v.shape[-1])
    sides = pltpu.roll(flat, 1, 1) + pltpu.roll(flat, flat.shape[1] - 1, 1)
    edge = jnp.zeros_like(v[:, :1])
    inward = jnp.concatenate([edge, v[:, :-1]], axis=1)
    outward = jnp.concatenate([v[:, 1:], edge], axis=1)
    return sides.reshape(v.shape) + (inward + outward)


def spread(row):
    return jnp.broadcast_to(row[:, :, None, None, :], row.shape[:2] + (1, 8, row.shape[2]))


def lookup(blocks, panel_rows):
    layers = []
    for l in range(panel_rows.shape[0]):
        out = []
        for r in range(panel_rows.shape[1]):
            where = jnp.broadcast_to(panel_rows[l, r : r + 1], (8, panel_rows.shape[2]))
            low = where & 127
            high = where >> 7
            hits = [high == j for j in range(1, len(blocks[0]))]
            halves = []
            for pieces in blocks:
                found = jnp.take_along_axis(pieces[0], low, axis=1)
                for j in range(1, len(pieces)):
                    found = jnp.where(hits[j - 1], jnp.take_along_axis(pieces[j], low, axis=1), found)
                halves.append(found)
            out.append(jnp.stack(halves))
        layers.append(jnp.stack(out))
    return jnp.stack(layers)


def chunked(low, high, step, body):
    whole = (high - low) // step

    def run(k, _):
        body(low, step * k, step)
        return 0

    lax.fori_loop(0, whole, run, 0)
    rest = (high - low) - whole * step
    if rest:
        body(low, whole * step, rest)


def vcycle_kernel(total, pressure_any, panel_any, flags_any, diagonal_any, fields, ext, loads, chunk_diag,
                  pressure, panel, flags, diagonal, arrive, b0, c0, v0a, v0b, r0, w0, d0, b1, c1, v1a, v1b, r1, w1, d1, b2, v2a, v2b, w2):
    slab = lax.axis_index("slab")
    group = lax.axis_index("case")
    own = fields.shape[1]
    pad = REACH * own
    cases = fields.shape[0]
    copies = [
        pltpu.make_async_copy(src, dst, arrive.at[n])
        for n, (src, dst) in enumerate(
            ((pressure_any, pressure), (panel_any, panel), (flags_any, flags), (diagonal_any, diagonal))
        )
    ]
    for copy in copies:
        copy.start()
    for copy in copies:
        copy.wait()
    first = pl.multiple_of(group * cases, cases)
    blocks = [
        [pressure[pl.ds(first + 8 * h, 8), 128 * j : 128 * j + 128] for j in range(pressure.shape[1] // 128)]
        for h in range(cases // 8)
    ]

    def inside(p, shape, level):
        g = lax.broadcasted_iota(jnp.int32, shape, 0) + (p + slab * (own >> level))
        return (g >= pad >> level) & (g < (total + pad) >> level)

    def span_of(p, shape):
        at = (lax.broadcasted_iota(jnp.int32, shape, 0) + (p + slab * own - pad)).astype(jnp.float32)
        return 1.0 + 2.0 * at / total

    def setup(low, k, n):
        p = k + (low + pad - BASE)
        here = pl.ds(k + low, n)
        held = flags[pl.ds(p, n)].astype(jnp.float32)
        coeff = diagonal[pl.ds(p, n)] + 4.0 * held
        c0[here] = coeff
        full = coeff + 6.0
        within = inside(p, full.shape, 0)
        w = spread(jnp.where(within, 0.7 / full, 0.0))
        factor = spread(jnp.where(within, (1.0 - held) * span_of(p, full.shape), 0.0))
        w0[here] = w
        d0[here] = spread(full)
        rhs = lookup(blocks, panel[pl.ds(p, n)]) * factor
        b0[here] = rhs
        v0a[here] = w * rhs

    chunked(0, 71, SETUP_STEP, setup)

    def swept(src, rhs, w, weight, at, n):
        wide = src[pl.ds(at - 1, n + 2)]
        v = wide[1:-1]
        near = wide[:-2] + wide[2:]
        if weight != 1.0:
            near = weight * near
        return 0.3 * v + w[pl.ds(at, n)] * (rhs[pl.ds(at, n)] + near + lateral(v))

    def sweep(src, dst, rhs, w, weight, base, low, high):
        def body(start, k, n):
            dst[pl.ds(k + start, n)] = swept(src, rhs, w, weight, k + start, n)

        chunked(low + base, high + base, SWEEP_STEP, body)

    def residual(src, dst, rhs, full, weight, base, low, high, level):
        def body(start, k, n):
            at = k + start
            wide = src[pl.ds(at - 1, n + 2)]
            v = wide[1:-1]
            near = wide[:-2] + wide[2:]
            if weight != 1.0:
                near = weight * near
            left = rhs[pl.ds(at, n)] - full[pl.ds(at, n)] * v + (near + lateral(v))
            for j in range(n):
                keep = inside(at + ((pad >> level) - base) + j, (1, 1, 1, 128), level)
                dst[at + j] = jnp.where(keep, left[j], 0.0)

        chunked(low + base, high + base, SWEEP_STEP, body)

    def restrict(fine, fine_base, cfine, rhs, ccoarse, w, full, vinit, weight, base, low, high, level):
        def body(start, k, n):
            for j in range(n):
                at = 2 * k + (fine_base + 2 * low + 2 * j)
                i = k + (start + j)
                value = 0.5 * fine[at] + 0.25 * (fine[at + 1] + fine[at - 1])
                coeff = 0.5 * (cfine[at] + cfine[at + 1])
                diag = coeff + (2.0 * weight + 4.0)
                if ccoarse is not None:
                    ccoarse[i] = coeff
                    full[i] = spread(diag[None])[0]
                keep = inside(k + (low + (pad >> level) + j), (1, 128), level)
                scale = spread(jnp.where(keep, 0.7 / diag, 0.0)[None])[0]
                w[i] = scale
                rhs[i] = value
                vinit[i] = scale * value

        chunked(low + base, high + base, COARSE_STEP, body)

    def prolong(coarse, coarse_base, v, base, low, high, level):
        def body(start, k, n):
            wide = coarse[pl.ds(k + start, n + 1)]
            between = 0.5 * (wide[:-1] + wide[1:])
            for j in range(n):
                at = 2 * k + (2 * low + base + 2 * j)
                p = 2 * k + (2 * low + (pad >> level) + 2 * j)
                keep = inside(p, (1, 1, 1, 128), level)
                v[at] = v[at] + jnp.where(keep, wide[j], 0.0)
                keep = inside(p + 1, (1, 1, 1, 128), level)
                v[at + 1] = v[at + 1] + jnp.where(keep, between[j], 0.0)

        chunked(low + coarse_base, high + coarse_base, COARSE_STEP, body)

    sweep(v0a, v0b, b0, w0, 1.0, BASE, -28, 41)
    residual(v0b, r0, b0, d0, 1.0, BASE, -27, 40, 0)
    restrict(r0, BASE, c0, b1, c1, w1, d1, v1a, 0.25, 14, -13, 20, 1)
    sweep(v1a, v1b, b1, w1, 0.25, 14, -12, 19)
    residual(v1b, r1, b1, d1, 0.25, 14, -11, 18, 1)
    restrict(r1, 14, c1, b2, None, w2, None, v2a, 0.0625, 6, -5, 9, 2)
    sweep(v2a, v2b, b2, w2, 0.0625, 6, -4, 8)
    sweep(v2b, v2a, b2, w2, 0.0625, 6, -3, 7)
    sweep(v2a, v2b, b2, w2, 0.0625, 6, -2, 6)
    prolong(v2b, 6, v1b, 14, -2, 5, 1)
    sweep(v1b, v1a, b1, w1, 0.25, 14, -3, 9)
    sweep(v1a, v1b, b1, w1, 0.25, 14, -2, 8)
    prolong(v1b, 14, v0b, BASE, -2, 7, 0)
    keep = inside(14 + pad, (1, 1, 1, 128), 0)
    v0b[14 + BASE] = v0b[14 + BASE] + jnp.where(keep[0], v1b[7 + 14], 0.0)
    sweep(v0b, v0a, b0, w0, 1.0, BASE, -2, 14)

    def last(start, k, n):
        ext[pl.ds(k + start, n)] = swept(v0a, b0, w0, 1.0, k + (start + BASE), n)

    chunked(0, own + 1, SWEEP_STEP, last)
    for f in range(own):
        for r in range(fields.shape[2]):
            fields[:, f, r, :] = ext[f, r].reshape(cases, 128)

    share = own // CASES
    every = [
        [pressure[8 * h : 8 * h + 8, 128 * k : 128 * k + 128] for k in range(pressure.shape[1] // 128)]
        for h in range(pressure.shape[0] // 8)
    ]
    for j in range(share):
        p = group * share + (pad + j)
        held = flags[pl.ds(p, 1)].astype(jnp.float32)
        factor = spread((1.0 - held) * span_of(p, held.shape))
        chunk_diag[pl.ds(j, 1)] = spread(diagonal[pl.ds(p, 1)] + 4.0 * held + 6.0)
        loads[pl.ds(j, 1)] = lookup(every, panel[pl.ds(p, 1)]) * factor


def solve(pressure, panel, flags, diagonal, total, own, radial, around, cases):
    halves = cases // 8
    vm = pl.BlockSpec(memory_space=pltpu.VMEM)
    share = own // CASES
    ext_shape = (own + 1, radial, halves, 8, around)

    def field(n):
        return pltpu.VMEM((n, radial, halves, 8, around), jnp.float32)

    def wide(n):
        return pltpu.VMEM((n, radial, 1, 8, around), jnp.float32)

    def plain(n):
        return pltpu.VMEM((n, radial, around), jnp.float32)

    return pl.pallas_call(
        functools.partial(vcycle_kernel, total),
        out_shape=[
            jax.ShapeDtypeStruct((cases, own, radial, around), jnp.float32),
            jax.ShapeDtypeStruct(ext_shape, jnp.float32),
            jax.ShapeDtypeStruct((share, radial, pressure.shape[0] // 8, 8, around), jnp.float32),
            jax.ShapeDtypeStruct((share, radial, 1, 8, around), jnp.float32),
        ],
        in_specs=[pl.BlockSpec(memory_space=pl.ANY)] * 4,
        out_specs=[vm] * 4,
        scratch_shapes=[
            pltpu.VMEM(pressure.shape, jnp.float32),
            pltpu.VMEM(panel.shape, jnp.int32),
            pltpu.VMEM(panel.shape, jnp.int32),
            pltpu.VMEM(panel.shape, jnp.float32),
            pltpu.SemaphoreType.DMA((4,)),
            field(72), plain(72), field(72), field(72), field(72), wide(72), wide(72),
            field(36), plain(36), field(36), field(36), field(36), wide(36), wide(36),
            field(16), field(16), field(16), wide(16),
        ],
        compiler_params=pltpu.CompilerParams(vmem_limit_bytes=64000000),
        name="vcycle",
    )(pressure, panel, flags, diagonal)


def gram_kernel(ext, loads_any, diag_any, gram, cross, loads, chunk_diag, pieces, rows, along_z, along_y,
                piece_send, piece_recv, row_send, row_recv, z_send, z_recv, y_send, y_recv, own_sem):
    slab = lax.axis_index("slab")
    group = lax.axis_index("case")
    core = lax.rem(slab, CORES)
    z = lax.rem(slab // CORES, ZSIZE)
    y = slab // (CORES * ZSIZE)
    pair = slab - core
    share = loads.shape[0]
    barrier = pltpu.get_barrier_semaphore()

    mates = [(dx, dc) for dc in range(CORES) for dx in range(CASES) if (dx, dc) != (0, 0)]

    def mate(dx, dc):
        return (pair + lax.rem(core + dc, CORES), lax.rem(group + dx, CASES))

    def z_mate(d):
        return (y * (ZSIZE * CORES) + lax.rem(z + d, ZSIZE) * CORES + core, group)

    def y_mate(d):
        return (lax.rem(y + d, YSIZE) * (ZSIZE * CORES) + z * CORES + core, group)

    everyone = [mate(dx, dc) for dx, dc in mates]
    everyone += [z_mate(d) for d in range(1, ZSIZE)]
    everyone += [y_mate(d) for d in range(1, YSIZE)]
    for device in everyone:
        pl.semaphore_signal(barrier, inc=1, device_id=device, device_id_type=MESH)
    keep = pltpu.make_async_copy(ext.at[pl.ds(group * share, share + 1)], pieces.at[group], own_sem.at[0])
    keep.start()
    load_copy = pltpu.make_async_copy(loads_any, loads, own_sem.at[1])
    load_copy.start()
    diag_copy = pltpu.make_async_copy(diag_any, chunk_diag, own_sem.at[2])
    diag_copy.start()
    pl.semaphore_wait(barrier, len(everyone))

    copies = []
    for dx in (2, 1, 3):
        there = lax.rem(group + dx, CASES)
        copy = pltpu.make_async_remote_copy(
            src_ref=ext.at[pl.ds(there * share, share + 1)],
            dst_ref=pieces.at[group],
            send_sem=piece_send.at[there],
            recv_sem=piece_recv.at[group],
            device_id=(slab, there),
            device_id_type=MESH,
        )
        copy.start()
        copies.append(copy)
    keep.wait()
    load_copy.wait()
    diag_copy.wait()
    for dx in (1, 2, 3):
        source = lax.rem(group + dx, CASES)
        pltpu.make_async_remote_copy(
            src_ref=pieces.at[source],
            dst_ref=pieces.at[source],
            send_sem=piece_send.at[source],
            recv_sem=piece_recv.at[source],
            device_id=(slab, source),
            device_id_type=MESH,
        ).wait_recv()

    radial, around = ext.shape[1], ext.shape[-1]
    image_parts, field_parts, above_parts, load_parts = [], [], [], []

    def rows_of(values, r):
        return jnp.concatenate([v[0, r].reshape(-1, around) for v in values], axis=0)

    for j in range(share):
        here = [pieces[g, j : j + 1] for g in range(CASES)]
        above = [pieces[g, j + 1 : j + 2] for g in range(CASES)]
        image = [chunk_diag[j : j + 1] * v - lateral(v) for v in here]
        for r in range(radial):
            image_parts.append(rows_of(image, r))
            field_parts.append(rows_of(here, r))
            above_parts.append(rows_of(above, r))
            load_parts.append(loads[j, r].reshape(-1, around))
    left = jnp.concatenate(
        [jnp.concatenate(parts, axis=1) for parts in (image_parts, above_parts, load_parts)], axis=0
    )
    right = jnp.concatenate(field_parts, axis=1)
    product = lax.dot_general(
        left, right, (((1,), (1,)), ((), ())), precision=highest, preferred_element_type=jnp.float32
    )
    count = right.shape[0]
    coupling = product[count : 2 * count]
    both = jnp.concatenate(
        [product[:count] - (coupling + coupling.T), product[2 * count :]], axis=1
    )
    per = count // CASES
    for g in range(CASES):
        rows[0, g] = both[g * per : (g + 1) * per]
    for dx, dc in mates:
        there_slab, there_group = mate(dx, dc)
        copy = pltpu.make_async_remote_copy(
            src_ref=rows.at[0, there_group],
            dst_ref=rows.at[1 + core, group],
            send_sem=row_send.at[dx, dc],
            recv_sem=row_recv.at[core, group],
            device_id=(there_slab, there_group),
            device_id_type=MESH,
        )
        copy.start()
        copies.append(copy)
    rows[1 + core, group] = rows[0, group]
    for dx, dc in mates:
        source_core, source_group = lax.rem(core + dc, CORES), lax.rem(group + dx, CASES)
        pltpu.make_async_remote_copy(
            src_ref=rows.at[1 + source_core, source_group],
            dst_ref=rows.at[1 + source_core, source_group],
            send_sem=row_send.at[dx, dc],
            recv_sem=row_recv.at[source_core, source_group],
            device_id=(slab, group),
            device_id_type=MESH,
        ).wait_recv()
    total = rows[1, 0]
    for c in range(CORES):
        for g in range(CASES):
            if (c, g) != (0, 0):
                total = total + rows[1 + c, g]

    def combine(total, slots, at, size, device, send, recv):
        slots[at] = total
        for d in range(1, size):
            copy = pltpu.make_async_remote_copy(
                src_ref=slots.at[at],
                dst_ref=slots.at[at],
                send_sem=send.at[d],
                recv_sem=recv.at[at],
                device_id=device(d),
                device_id_type=MESH,
            )
            copy.start()
            copies.append(copy)
        for d in range(1, size):
            source = lax.rem(at + d, size)
            pltpu.make_async_remote_copy(
                src_ref=slots.at[source],
                dst_ref=slots.at[source],
                send_sem=send.at[d],
                recv_sem=recv.at[source],
                device_id=device(d),
                device_id_type=MESH,
            ).wait_recv()
        result = slots[0]
        for d in range(1, size):
            result = result + slots[d]
        return result

    total = combine(total, along_z, z, ZSIZE, z_mate, z_send, z_recv)
    total = combine(total, along_y, y, YSIZE, y_mate, y_send, y_recv)
    gram[...] = total[:, :count]
    cross[...] = total[:, count:]
    for copy in copies:
        copy.wait_send()


def reduce_gram(ext, loads, chunk_diag, per):
    vm = pl.BlockSpec(memory_space=pltpu.VMEM)
    share = loads.shape[0]
    width = 2 * per * CASES
    return pl.pallas_call(
        gram_kernel,
        out_shape=[jax.ShapeDtypeStruct((per, width // 2), jnp.float32)] * 2,
        in_specs=[pl.BlockSpec(memory_space=pl.ANY)] * 3,
        out_specs=[vm] * 2,
        scratch_shapes=[
            pltpu.VMEM(loads.shape, jnp.float32),
            pltpu.VMEM(chunk_diag.shape, jnp.float32),
            pltpu.VMEM((CASES, share + 1) + ext.shape[1:], jnp.float32),
            pltpu.VMEM((1 + CORES, CASES, per, width), jnp.float32),
            pltpu.VMEM((ZSIZE, per, width), jnp.float32),
            pltpu.VMEM((YSIZE, per, width), jnp.float32),
            pltpu.SemaphoreType.DMA((CASES,)),
            pltpu.SemaphoreType.DMA((CASES,)),
            pltpu.SemaphoreType.DMA((CASES, CORES)),
            pltpu.SemaphoreType.DMA((CORES, CASES)),
            pltpu.SemaphoreType.DMA((ZSIZE,)),
            pltpu.SemaphoreType.DMA((ZSIZE,)),
            pltpu.SemaphoreType.DMA((YSIZE,)),
            pltpu.SemaphoreType.DMA((YSIZE,)),
            pltpu.SemaphoreType.DMA((3,)),
        ],
        compiler_params=pltpu.CompilerParams(collective_id=2, has_side_effects=True, vmem_limit_bytes=64000000),
        name="gram",
    )(ext, loads, chunk_diag)


def local(pressure, panel, flags, diagonal):
    layers, radial, around = panel.shape
    slabs = lax.axis_size("slab")
    groups = lax.axis_size("case")
    per = pressure.shape[0] // groups
    total = layers * slabs
    spreads = exchange_halo(panel, flags, diagonal, slabs)
    wide = [x.reshape((-1,) + panel.shape[1:]) for x in spreads]
    fields, ext, loads, chunk_diag = solve(pressure, *wide, total, layers, radial, around, per)
    gram, cross = reduce_gram(ext, loads, chunk_diag, per)
    scale = 1.0 / (total * radial * around)
    return (fields, gram * scale, cross * scale)


def solution(mesh):
    in_specs = (P(), P("slab", None, None), P("slab", None, None), P("slab", None, None))
    out_specs = (P("case", "slab", None, None), P("case", None), P("case", None))
    return jax.shard_map(local, mesh=mesh, in_specs=in_specs, out_specs=out_specs, check_vma=False)
```

```python
import functools

import jax
import jax.numpy as jnp
from jax import lax
from jax.experimental import pallas as pl
from jax.experimental.pallas import tpu as pltpu
from jax.sharding import PartitionSpec as P

MESH = pl.DeviceIdType.MESH
ZSIZE = 8
YSIZE = 8
CORES = 2
CASES = 4
REACH = 3
BASE = 29
SETUP_STEP = 18
SWEEP_STEP = 36
COARSE_STEP = 11
highest = lax.Precision.HIGHEST


def halo_kernel(slabs, panel, flags, diagonal, panel_out, flags_out, diagonal_out, send, recv, own):
    slab = lax.axis_index("slab")
    barrier = pltpu.get_barrier_semaphore()
    shifts = [d for d in range(-REACH, REACH + 1) if d != 0]
    for d in shifts:
        there = lax.rem(slab + d + slabs, slabs)
        pl.semaphore_signal(barrier, inc=1, device_id={"slab": there}, device_id_type=MESH)
    locals_ = []
    for n, (src, dst) in enumerate(((panel, panel_out), (flags, flags_out), (diagonal, diagonal_out))):
        copy = pltpu.make_async_copy(src, dst.at[REACH], own.at[n])
        copy.start()
        locals_.append(copy)
    pl.semaphore_wait(barrier, len(shifts))
    copies = []
    layers = panel.shape[0]
    for d in sorted(shifts, key=lambda d: -abs(d)):
        there = lax.rem(slab + d + slabs, slabs)
        slot = REACH - d
        start, count = {3: (layers - 5, 5), -3: (0, 6)}.get(d, (0, layers))
        for n, (src, dst) in enumerate(((panel, panel_out), (flags, flags_out), (diagonal, diagonal_out))):
            copy = pltpu.make_async_remote_copy(
                src_ref=src.at[pl.ds(start, count)],
                dst_ref=dst.at[slot, pl.ds(start, count)],
                send_sem=send.at[n, slot],
                recv_sem=recv.at[n, slot],
                device_id={"slab": there},
                device_id_type=MESH,
            )
            copy.start()
            copies.append(copy)
    for copy in locals_:
        copy.wait()
    for copy in copies:
        copy.wait()


def exchange_halo(panel, flags, diagonal, slabs):
    shape = (2 * REACH + 1,) + panel.shape
    anyspace = pl.BlockSpec(memory_space=pl.ANY)
    return pl.pallas_call(
        functools.partial(halo_kernel, slabs),
        out_shape=[
            jax.ShapeDtypeStruct(shape, jnp.int32),
            jax.ShapeDtypeStruct(shape, jnp.int32),
            jax.ShapeDtypeStruct(shape, jnp.float32),
        ],
        in_specs=[anyspace] * 3,
        out_specs=[anyspace] * 3,
        scratch_shapes=[
            pltpu.SemaphoreType.DMA((3, 2 * REACH + 1)),
            pltpu.SemaphoreType.DMA((3, 2 * REACH + 1)),
            pltpu.SemaphoreType.DMA((3,)),
        ],
        compiler_params=pltpu.CompilerParams(collective_id=1, has_side_effects=True),
        name="halo",
    )(panel, flags, diagonal)


def lateral(v):
    flat = v.reshape(-1, v.shape[-1])
    sides = pltpu.roll(flat, 1, 1) + pltpu.roll(flat, flat.shape[1] - 1, 1)
    edge = jnp.zeros_like(v[:, :1])
    inward = jnp.concatenate([edge, v[:, :-1]], axis=1)
    outward = jnp.concatenate([v[:, 1:], edge], axis=1)
    return sides.reshape(v.shape) + (inward + outward)


def spread(row):
    return jnp.broadcast_to(row[:, :, None, None, :], row.shape[:2] + (1, 8, row.shape[2]))


def lookup(blocks, panel_rows):
    layers = []
    for l in range(panel_rows.shape[0]):
        out = []
        for r in range(panel_rows.shape[1]):
            where = jnp.broadcast_to(panel_rows[l, r : r + 1], (8, panel_rows.shape[2]))
            low = where & 127
            high = where >> 7
            hits = [high == j for j in range(1, len(blocks[0]))]
            halves = []
            for pieces in blocks:
                found = jnp.take_along_axis(pieces[0], low, axis=1)
                for j in range(1, len(pieces)):
                    found = jnp.where(hits[j - 1], jnp.take_along_axis(pieces[j], low, axis=1), found)
                halves.append(found)
            out.append(jnp.stack(halves))
        layers.append(jnp.stack(out))
    return jnp.stack(layers)


def chunked(low, high, step, body):
    whole = (high - low) // step

    def run(k, _):
        body(low, step * k, step)
        return 0

    lax.fori_loop(0, whole, run, 0)
    rest = (high - low) - whole * step
    if rest:
        body(low, whole * step, rest)


def step_kernel(total, pressure_any, panel_any, flags_any, diagonal_any, fields_any, gram, cross,
                fields, field_sem, loads, chunk_diag, pieces, rows, along_z, along_y,
                piece_send, piece_recv, row_send, row_recv, z_send, z_recv, y_send, y_recv, own_sem,
                ext, pressure, panel, flags, diagonal, arrive, b0, c0, v0a, v0b, r0, w0, d0, b1, c1, v1a, v1b, r1, w1, d1, b2, v2a, v2b, w2):
    slab = lax.axis_index("slab")
    group = lax.axis_index("case")
    own = fields.shape[1]
    pad = REACH * own
    cases = fields.shape[0]
    core = lax.rem(slab, CORES)
    z = lax.rem(slab // CORES, ZSIZE)
    y = slab // (CORES * ZSIZE)
    pair = slab - core
    share = loads.shape[0]
    barrier = pltpu.get_barrier_semaphore()

    mates = [(dx, dc) for dc in range(CORES) for dx in range(CASES) if (dx, dc) != (0, 0)]

    def mate(dx, dc):
        return (pair + lax.rem(core + dc, CORES), lax.rem(group + dx, CASES))

    def z_mate(d):
        return (y * (ZSIZE * CORES) + lax.rem(z + d, ZSIZE) * CORES + core, group)

    def y_mate(d):
        return (lax.rem(y + d, YSIZE) * (ZSIZE * CORES) + z * CORES + core, group)

    everyone = [mate(dx, dc) for dx, dc in mates]
    everyone += [z_mate(d) for d in range(1, ZSIZE)]
    everyone += [y_mate(d) for d in range(1, YSIZE)]
    for device in everyone:
        pl.semaphore_signal(barrier, inc=1, device_id=device, device_id_type=MESH)
    copies = [
        pltpu.make_async_copy(src, dst, arrive.at[n])
        for n, (src, dst) in enumerate(
            ((pressure_any, pressure), (panel_any, panel), (flags_any, flags), (diagonal_any, diagonal))
        )
    ]
    for copy in copies:
        copy.start()
    for copy in copies:
        copy.wait()
    first = pl.multiple_of(group * cases, cases)
    blocks = [
        [pressure[pl.ds(first + 8 * h, 8), 128 * j : 128 * j + 128] for j in range(pressure.shape[1] // 128)]
        for h in range(cases // 8)
    ]

    def inside(p, shape, level):
        g = lax.broadcasted_iota(jnp.int32, shape, 0) + (p + slab * (own >> level))
        return (g >= pad >> level) & (g < (total + pad) >> level)

    def span_of(p, shape):
        at = (lax.broadcasted_iota(jnp.int32, shape, 0) + (p + slab * own - pad)).astype(jnp.float32)
        return 1.0 + 2.0 * at / total

    def setup(low, k, n):
        p = k + (low + pad - BASE)
        here = pl.ds(k + low, n)
        held = flags[pl.ds(p, n)].astype(jnp.float32)
        coeff = diagonal[pl.ds(p, n)] + 4.0 * held
        c0[here] = coeff
        full = coeff + 6.0
        within = inside(p, full.shape, 0)
        w = spread(jnp.where(within, 0.7 / full, 0.0))
        factor = spread(jnp.where(within, (1.0 - held) * span_of(p, full.shape), 0.0))
        w0[here] = w
        d0[here] = spread(full)
        rhs = lookup(blocks, panel[pl.ds(p, n)]) * factor
        b0[here] = rhs
        v0a[here] = w * rhs

    chunked(0, 71, SETUP_STEP, setup)

    def swept(src, rhs, w, weight, at, n):
        wide = src[pl.ds(at - 1, n + 2)]
        v = wide[1:-1]
        near = wide[:-2] + wide[2:]
        if weight != 1.0:
            near = weight * near
        return 0.3 * v + w[pl.ds(at, n)] * (rhs[pl.ds(at, n)] + near + lateral(v))

    def sweep(src, dst, rhs, w, weight, base, low, high):
        def body(start, k, n):
            dst[pl.ds(k + start, n)] = swept(src, rhs, w, weight, k + start, n)

        chunked(low + base, high + base, SWEEP_STEP, body)

    def residual(src, dst, rhs, full, weight, base, low, high, level):
        def body(start, k, n):
            at = k + start
            wide = src[pl.ds(at - 1, n + 2)]
            v = wide[1:-1]
            near = wide[:-2] + wide[2:]
            if weight != 1.0:
                near = weight * near
            left = rhs[pl.ds(at, n)] - full[pl.ds(at, n)] * v + (near + lateral(v))
            for j in range(n):
                keep = inside(at + ((pad >> level) - base) + j, (1, 1, 1, 128), level)
                dst[at + j] = jnp.where(keep, left[j], 0.0)

        chunked(low + base, high + base, SWEEP_STEP, body)

    def restrict(fine, fine_base, cfine, rhs, ccoarse, w, full, vinit, weight, base, low, high, level):
        def body(start, k, n):
            for j in range(n):
                at = 2 * k + (fine_base + 2 * low + 2 * j)
                i = k + (start + j)
                value = 0.5 * fine[at] + 0.25 * (fine[at + 1] + fine[at - 1])
                coeff = 0.5 * (cfine[at] + cfine[at + 1])
                diag = coeff + (2.0 * weight + 4.0)
                if ccoarse is not None:
                    ccoarse[i] = coeff
                    full[i] = spread(diag[None])[0]
                keep = inside(k + (low + (pad >> level) + j), (1, 128), level)
                scale = spread(jnp.where(keep, 0.7 / diag, 0.0)[None])[0]
                w[i] = scale
                rhs[i] = value
                vinit[i] = scale * value

        chunked(low + base, high + base, COARSE_STEP, body)

    def prolong(coarse, coarse_base, v, base, low, high, level):
        def body(start, k, n):
            wide = coarse[pl.ds(k + start, n + 1)]
            between = 0.5 * (wide[:-1] + wide[1:])
            for j in range(n):
                at = 2 * k + (2 * low + base + 2 * j)
                p = 2 * k + (2 * low + (pad >> level) + 2 * j)
                keep = inside(p, (1, 1, 1, 128), level)
                v[at] = v[at] + jnp.where(keep, wide[j], 0.0)
                keep = inside(p + 1, (1, 1, 1, 128), level)
                v[at + 1] = v[at + 1] + jnp.where(keep, between[j], 0.0)

        chunked(low + coarse_base, high + coarse_base, COARSE_STEP, body)

    sweep(v0a, v0b, b0, w0, 1.0, BASE, -28, 41)
    residual(v0b, r0, b0, d0, 1.0, BASE, -27, 40, 0)
    restrict(r0, BASE, c0, b1, c1, w1, d1, v1a, 0.25, 14, -13, 20, 1)
    sweep(v1a, v1b, b1, w1, 0.25, 14, -12, 19)
    residual(v1b, r1, b1, d1, 0.25, 14, -11, 18, 1)
    restrict(r1, 14, c1, b2, None, w2, None, v2a, 0.0625, 6, -5, 9, 2)
    sweep(v2a, v2b, b2, w2, 0.0625, 6, -4, 8)
    sweep(v2b, v2a, b2, w2, 0.0625, 6, -3, 7)
    sweep(v2a, v2b, b2, w2, 0.0625, 6, -2, 6)
    prolong(v2b, 6, v1b, 14, -2, 5, 1)
    sweep(v1b, v1a, b1, w1, 0.25, 14, -3, 9)
    sweep(v1a, v1b, b1, w1, 0.25, 14, -2, 8)
    prolong(v1b, 14, v0b, BASE, -2, 7, 0)
    keep = inside(14 + pad, (1, 1, 1, 128), 0)
    v0b[14 + BASE] = v0b[14 + BASE] + jnp.where(keep[0], v1b[7 + 14], 0.0)
    sweep(v0b, v0a, b0, w0, 1.0, BASE, -2, 14)

    def last(start, k, n):
        ext[pl.ds(k + start, n)] = swept(v0a, b0, w0, 1.0, k + (start + BASE), n)

    chunked(0, own + 1, SWEEP_STEP, last)
    keep = pltpu.make_async_copy(ext.at[pl.ds(group * share, share + 1)], pieces.at[group], own_sem)
    keep.start()
    pl.semaphore_wait(barrier, len(everyone))
    sent = []
    for dx in (2, 1, 3):
        there = lax.rem(group + dx, CASES)
        copy = pltpu.make_async_remote_copy(
            src_ref=ext.at[pl.ds(there * share, share + 1)],
            dst_ref=pieces.at[group],
            send_sem=piece_send.at[there],
            recv_sem=piece_recv.at[group],
            device_id=(slab, there),
            device_id_type=MESH,
        )
        copy.start()
        sent.append(copy)
    for f in range(own):
        for r in range(fields.shape[2]):
            fields[:, f, r, :] = ext[f, r].reshape(cases, 128)

    field_copy = pltpu.make_async_copy(fields, fields_any, field_sem)
    field_copy.start()
    every = [
        [pressure[8 * h : 8 * h + 8, 128 * k : 128 * k + 128] for k in range(pressure.shape[1] // 128)]
        for h in range(pressure.shape[0] // 8)
    ]
    for j in range(share):
        p = group * share + (pad + j)
        held = flags[pl.ds(p, 1)].astype(jnp.float32)
        factor = spread((1.0 - held) * span_of(p, held.shape))
        chunk_diag[pl.ds(j, 1)] = spread(diagonal[pl.ds(p, 1)] + 4.0 * held + 6.0)
        loads[pl.ds(j, 1)] = lookup(every, panel[pl.ds(p, 1)]) * factor

    keep.wait()
    for dx in (1, 2, 3):
        source = lax.rem(group + dx, CASES)
        pltpu.make_async_remote_copy(
            src_ref=pieces.at[source],
            dst_ref=pieces.at[source],
            send_sem=piece_send.at[source],
            recv_sem=piece_recv.at[source],
            device_id=(slab, source),
            device_id_type=MESH,
        ).wait_recv()

    radial, around = ext.shape[1], ext.shape[-1]
    image_parts, field_parts, above_parts, load_parts = [], [], [], []

    def rows_of(values, r):
        return jnp.concatenate([v[0, r].reshape(-1, around) for v in values], axis=0)

    for j in range(share):
        here = [pieces[g, j : j + 1] for g in range(CASES)]
        above = [pieces[g, j + 1 : j + 2] for g in range(CASES)]
        image = [chunk_diag[j : j + 1] * v - lateral(v) for v in here]
        for r in range(radial):
            image_parts.append(rows_of(image, r))
            field_parts.append(rows_of(here, r))
            above_parts.append(rows_of(above, r))
            load_parts.append(loads[j, r].reshape(-1, around))
    left = jnp.concatenate(
        [jnp.concatenate(parts, axis=1) for parts in (image_parts, above_parts, load_parts)], axis=0
    )
    right = jnp.concatenate(field_parts, axis=1)
    product = lax.dot_general(
        left, right, (((1,), (1,)), ((), ())), precision=highest, preferred_element_type=jnp.float32
    )
    count = right.shape[0]
    coupling = product[count : 2 * count]
    both = jnp.concatenate(
        [product[:count] - (coupling + coupling.T), product[2 * count :]], axis=1
    )
    per = count // CASES
    for g in range(CASES):
        rows[0, g] = both[g * per : (g + 1) * per]
    for dx, dc in mates:
        there_slab, there_group = mate(dx, dc)
        copy = pltpu.make_async_remote_copy(
            src_ref=rows.at[0, there_group],
            dst_ref=rows.at[1 + core, group],
            send_sem=row_send.at[dx, dc],
            recv_sem=row_recv.at[core, group],
            device_id=(there_slab, there_group),
            device_id_type=MESH,
        )
        copy.start()
        sent.append(copy)
    rows[1 + core, group] = rows[0, group]
    for dx, dc in mates:
        source_core, source_group = lax.rem(core + dc, CORES), lax.rem(group + dx, CASES)
        pltpu.make_async_remote_copy(
            src_ref=rows.at[1 + source_core, source_group],
            dst_ref=rows.at[1 + source_core, source_group],
            send_sem=row_send.at[dx, dc],
            recv_sem=row_recv.at[source_core, source_group],
            device_id=(slab, group),
            device_id_type=MESH,
        ).wait_recv()
    total = rows[1, 0]
    for c in range(CORES):
        for g in range(CASES):
            if (c, g) != (0, 0):
                total = total + rows[1 + c, g]

    def combine(total, slots, at, size, device, send, recv):
        slots[at] = total
        for d in range(1, size):
            copy = pltpu.make_async_remote_copy(
                src_ref=slots.at[at],
                dst_ref=slots.at[at],
                send_sem=send.at[d],
                recv_sem=recv.at[at],
                device_id=device(d),
                device_id_type=MESH,
            )
            copy.start()
            sent.append(copy)
        for d in range(1, size):
            source = lax.rem(at + d, size)
            pltpu.make_async_remote_copy(
                src_ref=slots.at[source],
                dst_ref=slots.at[source],
                send_sem=send.at[d],
                recv_sem=recv.at[source],
                device_id=device(d),
                device_id_type=MESH,
            ).wait_recv()
        result = slots[0]
        for d in range(1, size):
            result = result + slots[d]
        return result

    total = combine(total, along_z, z, ZSIZE, z_mate, z_send, z_recv)
    total = combine(total, along_y, y, YSIZE, y_mate, y_send, y_recv)
    gram[...] = total[:, :count]
    cross[...] = total[:, count:]
    for copy in sent:
        copy.wait_send()
    field_copy.wait()


def solve(pressure, panel, flags, diagonal, total, own, radial, around, cases):
    halves = cases // 8
    share = own // CASES
    width = 2 * cases * CASES
    anyspace = pl.BlockSpec(memory_space=pl.ANY)
    vm = pl.BlockSpec(memory_space=pltpu.VMEM)

    def field(n):
        return pltpu.VMEM((n, radial, halves, 8, around), jnp.float32)

    def wide(n):
        return pltpu.VMEM((n, radial, 1, 8, around), jnp.float32)

    def plain(n):
        return pltpu.VMEM((n, radial, around), jnp.float32)

    return pl.pallas_call(
        functools.partial(step_kernel, total),
        out_shape=[
            jax.ShapeDtypeStruct((cases, own, radial, around), jnp.float32),
            jax.ShapeDtypeStruct((cases, width // 2), jnp.float32),
            jax.ShapeDtypeStruct((cases, width // 2), jnp.float32),
        ],
        in_specs=[anyspace] * 4,
        out_specs=[anyspace, vm, vm],
        scratch_shapes=[
            pltpu.VMEM((cases, own, radial, around), jnp.float32),
            pltpu.SemaphoreType.DMA,
            pltpu.VMEM((share, radial, pressure.shape[0] // 8, 8, around), jnp.float32),
            wide(share),
            pltpu.VMEM((CASES, share + 1, radial, halves, 8, around), jnp.float32),
            pltpu.VMEM((1 + CORES, CASES, cases, width), jnp.float32),
            pltpu.VMEM((ZSIZE, cases, width), jnp.float32),
            pltpu.VMEM((YSIZE, cases, width), jnp.float32),
            pltpu.SemaphoreType.DMA((CASES,)),
            pltpu.SemaphoreType.DMA((CASES,)),
            pltpu.SemaphoreType.DMA((CASES, CORES)),
            pltpu.SemaphoreType.DMA((CORES, CASES)),
            pltpu.SemaphoreType.DMA((ZSIZE,)),
            pltpu.SemaphoreType.DMA((ZSIZE,)),
            pltpu.SemaphoreType.DMA((YSIZE,)),
            pltpu.SemaphoreType.DMA((YSIZE,)),
            pltpu.SemaphoreType.DMA,
            field(own + 1),
            pltpu.VMEM(pressure.shape, jnp.float32),
            pltpu.VMEM(panel.shape, jnp.int32),
            pltpu.VMEM(panel.shape, jnp.int32),
            pltpu.VMEM(panel.shape, jnp.float32),
            pltpu.SemaphoreType.DMA((4,)),
            field(72), plain(72), field(72), field(72), field(72), wide(72), wide(72),
            field(36), plain(36), field(36), field(36), field(36), wide(36), wide(36),
            field(16), field(16), field(16), wide(16),
        ],
        compiler_params=pltpu.CompilerParams(
            collective_id=2, has_side_effects=True, vmem_limit_bytes=64000000
        ),
        name="step",
    )(pressure, panel, flags, diagonal)


def local(pressure, panel, flags, diagonal):
    layers, radial, around = panel.shape
    slabs = lax.axis_size("slab")
    groups = lax.axis_size("case")
    per = pressure.shape[0] // groups
    total = layers * slabs
    spreads = exchange_halo(panel, flags, diagonal, slabs)
    wide = [x.reshape((-1,) + panel.shape[1:]) for x in spreads]
    fields, gram, cross = solve(pressure, *wide, total, layers, radial, around, per)
    scale = 1.0 / (total * radial * around)
    return (fields, gram * scale, cross * scale)


def solution(mesh):
    in_specs = (P(), P("slab", None, None), P("slab", None, None), P("slab", None, None))
    out_specs = (P("case", "slab", None, None), P("case", None), P("case", None))
    return jax.shard_map(local, mesh=mesh, in_specs=in_specs, out_specs=out_specs, check_vma=False)
```

```python
import functools

import jax
import jax.numpy as jnp
from jax import lax
from jax.experimental import pallas as pl
from jax.experimental.pallas import tpu as pltpu
from jax.sharding import PartitionSpec as P

MESH = pl.DeviceIdType.MESH
ZSIZE = 8
YSIZE = 8
CORES = 2
CASES = 4
REACH = 3
BASE = 29
SETUP_STEP = 18
SWEEP_STEP = 36
COARSE_STEP = 11
highest = lax.Precision.HIGHEST


def halo_kernel(slabs, panel, flags, diagonal, panel_out, flags_out, diagonal_out, send, recv, own):
    slab = lax.axis_index("slab")
    barrier = pltpu.get_barrier_semaphore()
    shifts = [d for d in range(-REACH, REACH + 1) if d != 0]
    for d in shifts:
        there = lax.rem(slab + d + slabs, slabs)
        pl.semaphore_signal(barrier, inc=1, device_id={"slab": there}, device_id_type=MESH)
    locals_ = []
    for n, (src, dst) in enumerate(((panel, panel_out), (flags, flags_out), (diagonal, diagonal_out))):
        copy = pltpu.make_async_copy(src, dst.at[REACH], own.at[n])
        copy.start()
        locals_.append(copy)
    pl.semaphore_wait(barrier, len(shifts))
    copies = []
    layers = panel.shape[0]
    for d in sorted(shifts, key=lambda d: -abs(d)):
        there = lax.rem(slab + d + slabs, slabs)
        slot = REACH - d
        start, count = {3: (layers - 5, 5), -3: (0, 6)}.get(d, (0, layers))
        for n, (src, dst) in enumerate(((panel, panel_out), (flags, flags_out), (diagonal, diagonal_out))):
            copy = pltpu.make_async_remote_copy(
                src_ref=src.at[pl.ds(start, count)],
                dst_ref=dst.at[slot, pl.ds(start, count)],
                send_sem=send.at[n, slot],
                recv_sem=recv.at[n, slot],
                device_id={"slab": there},
                device_id_type=MESH,
            )
            copy.start()
            copies.append(copy)
    for copy in locals_:
        copy.wait()
    for copy in copies:
        copy.wait()


def exchange_halo(panel, flags, diagonal, slabs):
    shape = (2 * REACH + 1,) + panel.shape
    anyspace = pl.BlockSpec(memory_space=pl.ANY)
    return pl.pallas_call(
        functools.partial(halo_kernel, slabs),
        out_shape=[
            jax.ShapeDtypeStruct(shape, jnp.int32),
            jax.ShapeDtypeStruct(shape, jnp.int32),
            jax.ShapeDtypeStruct(shape, jnp.float32),
        ],
        in_specs=[anyspace] * 3,
        out_specs=[anyspace] * 3,
        scratch_shapes=[
            pltpu.SemaphoreType.DMA((3, 2 * REACH + 1)),
            pltpu.SemaphoreType.DMA((3, 2 * REACH + 1)),
            pltpu.SemaphoreType.DMA((3,)),
        ],
        compiler_params=pltpu.CompilerParams(collective_id=1, has_side_effects=True),
        name="halo",
    )(panel, flags, diagonal)


def lateral(v):
    flat = v.reshape(-1, v.shape[-1])
    sides = pltpu.roll(flat, 1, 1) + pltpu.roll(flat, flat.shape[1] - 1, 1)
    edge = jnp.zeros_like(v[:, :1])
    inward = jnp.concatenate([edge, v[:, :-1]], axis=1)
    outward = jnp.concatenate([v[:, 1:], edge], axis=1)
    return sides.reshape(v.shape) + (inward + outward)


def spread(row):
    return jnp.broadcast_to(row[:, :, None, None, :], row.shape[:2] + (1, 8, row.shape[2]))


def lookup(blocks, panel_rows):
    layers = []
    for l in range(panel_rows.shape[0]):
        out = []
        for r in range(panel_rows.shape[1]):
            where = jnp.broadcast_to(panel_rows[l, r : r + 1], (8, panel_rows.shape[2]))
            low = where & 127
            high = where >> 7
            hits = [high == j for j in range(1, len(blocks[0]))]
            halves = []
            for pieces in blocks:
                found = jnp.take_along_axis(pieces[0], low, axis=1)
                for j in range(1, len(pieces)):
                    found = jnp.where(hits[j - 1], jnp.take_along_axis(pieces[j], low, axis=1), found)
                halves.append(found)
            out.append(jnp.stack(halves))
        layers.append(jnp.stack(out))
    return jnp.stack(layers)


def chunked(low, high, step, body):
    whole = (high - low) // step

    def run(k, _):
        body(low, step * k, step)
        return 0

    lax.fori_loop(0, whole, run, 0)
    rest = (high - low) - whole * step
    if rest:
        body(low, whole * step, rest)


def step_kernel(total, pressure_any, panel_any, flags_any, diagonal_any, fields_any, gram, cross,
                fields, field_sem, loads, chunk_diag, pieces, rows, along_z, along_y,
                relay, relay_sems, piece_send, piece_recv, row_send, row_recv, z_send, z_recv, y_send, y_recv, own_sem,
                ext, pressure, panel, flags, diagonal, arrive, b0, c0, v0a, v0b, r0, w0, d0, b1, c1, v1a, v1b, r1, w1, d1, b2, v2a, v2b, w2):
    slab = lax.axis_index("slab")
    group = lax.axis_index("case")
    own = fields.shape[1]
    pad = REACH * own
    cases = fields.shape[0]
    core = lax.rem(slab, CORES)
    z = lax.rem(slab // CORES, ZSIZE)
    y = slab // (CORES * ZSIZE)
    pair = slab - core
    share = loads.shape[0]
    barrier = pltpu.get_barrier_semaphore()

    mates = [(dx, dc) for dc in range(CORES) for dx in range(CASES) if (dx, dc) != (0, 0)]

    def mate(dx, dc):
        return (pair + lax.rem(core + dc, CORES), lax.rem(group + dx, CASES))

    def z_mate(d):
        return (y * (ZSIZE * CORES) + lax.rem(z + d, ZSIZE) * CORES + core, group)

    def y_mate(d):
        return (lax.rem(y + d, YSIZE) * (ZSIZE * CORES) + z * CORES + core, group)

    everyone = [mate(dx, dc) for dx, dc in mates]
    everyone += [z_mate(d) for d in range(1, ZSIZE)]
    everyone += [y_mate(d) for d in range(1, YSIZE)]
    for device in everyone:
        pl.semaphore_signal(barrier, inc=1, device_id=device, device_id_type=MESH)
    copies = [
        pltpu.make_async_copy(src, dst, arrive.at[n])
        for n, (src, dst) in enumerate(
            ((pressure_any, pressure), (panel_any, panel), (flags_any, flags), (diagonal_any, diagonal))
        )
    ]
    for copy in copies:
        copy.start()
    for copy in copies:
        copy.wait()
    first = pl.multiple_of(group * cases, cases)
    blocks = [
        [pressure[pl.ds(first + 8 * h, 8), 128 * j : 128 * j + 128] for j in range(pressure.shape[1] // 128)]
        for h in range(cases // 8)
    ]

    def inside(p, shape, level):
        g = lax.broadcasted_iota(jnp.int32, shape, 0) + (p + slab * (own >> level))
        return (g >= pad >> level) & (g < (total + pad) >> level)

    def span_of(p, shape):
        at = (lax.broadcasted_iota(jnp.int32, shape, 0) + (p + slab * own - pad)).astype(jnp.float32)
        return 1.0 + 2.0 * at / total

    def setup(low, k, n):
        p = k + (low + pad - BASE)
        here = pl.ds(k + low, n)
        held = flags[pl.ds(p, n)].astype(jnp.float32)
        coeff = diagonal[pl.ds(p, n)] + 4.0 * held
        c0[here] = coeff
        full = coeff + 6.0
        within = inside(p, full.shape, 0)
        w = spread(jnp.where(within, 0.7 / full, 0.0))
        factor = spread(jnp.where(within, (1.0 - held) * span_of(p, full.shape), 0.0))
        w0[here] = w
        d0[here] = spread(full)
        rhs = lookup(blocks, panel[pl.ds(p, n)]) * factor
        b0[here] = rhs
        v0a[here] = w * rhs

    chunked(0, 71, SETUP_STEP, setup)

    def swept(src, rhs, w, weight, at, n):
        wide = src[pl.ds(at - 1, n + 2)]
        v = wide[1:-1]
        near = wide[:-2] + wide[2:]
        if weight != 1.0:
            near = weight * near
        return 0.3 * v + w[pl.ds(at, n)] * (rhs[pl.ds(at, n)] + near + lateral(v))

    def sweep(src, dst, rhs, w, weight, base, low, high):
        def body(start, k, n):
            dst[pl.ds(k + start, n)] = swept(src, rhs, w, weight, k + start, n)

        chunked(low + base, high + base, SWEEP_STEP, body)

    def residual(src, dst, rhs, full, weight, base, low, high, level):
        def body(start, k, n):
            at = k + start
            wide = src[pl.ds(at - 1, n + 2)]
            v = wide[1:-1]
            near = wide[:-2] + wide[2:]
            if weight != 1.0:
                near = weight * near
            left = rhs[pl.ds(at, n)] - full[pl.ds(at, n)] * v + (near + lateral(v))
            for j in range(n):
                keep = inside(at + ((pad >> level) - base) + j, (1, 1, 1, 128), level)
                dst[at + j] = jnp.where(keep, left[j], 0.0)

        chunked(low + base, high + base, SWEEP_STEP, body)

    def restrict(fine, fine_base, cfine, rhs, ccoarse, w, full, vinit, weight, base, low, high, level):
        def body(start, k, n):
            for j in range(n):
                at = 2 * k + (fine_base + 2 * low + 2 * j)
                i = k + (start + j)
                value = 0.5 * fine[at] + 0.25 * (fine[at + 1] + fine[at - 1])
                coeff = 0.5 * (cfine[at] + cfine[at + 1])
                diag = coeff + (2.0 * weight + 4.0)
                if ccoarse is not None:
                    ccoarse[i] = coeff
                    full[i] = spread(diag[None])[0]
                keep = inside(k + (low + (pad >> level) + j), (1, 128), level)
                scale = spread(jnp.where(keep, 0.7 / diag, 0.0)[None])[0]
                w[i] = scale
                rhs[i] = value
                vinit[i] = scale * value

        chunked(low + base, high + base, COARSE_STEP, body)

    def prolong(coarse, coarse_base, v, base, low, high, level):
        def body(start, k, n):
            wide = coarse[pl.ds(k + start, n + 1)]
            between = 0.5 * (wide[:-1] + wide[1:])
            for j in range(n):
                at = 2 * k + (2 * low + base + 2 * j)
                p = 2 * k + (2 * low + (pad >> level) + 2 * j)
                keep = inside(p, (1, 1, 1, 128), level)
                v[at] = v[at] + jnp.where(keep, wide[j], 0.0)
                keep = inside(p + 1, (1, 1, 1, 128), level)
                v[at + 1] = v[at + 1] + jnp.where(keep, between[j], 0.0)

        chunked(low + coarse_base, high + coarse_base, COARSE_STEP, body)

    sweep(v0a, v0b, b0, w0, 1.0, BASE, -28, 41)
    residual(v0b, r0, b0, d0, 1.0, BASE, -27, 40, 0)
    restrict(r0, BASE, c0, b1, c1, w1, d1, v1a, 0.25, 14, -13, 20, 1)
    sweep(v1a, v1b, b1, w1, 0.25, 14, -12, 19)
    residual(v1b, r1, b1, d1, 0.25, 14, -11, 18, 1)
    restrict(r1, 14, c1, b2, None, w2, None, v2a, 0.0625, 6, -5, 9, 2)
    sweep(v2a, v2b, b2, w2, 0.0625, 6, -4, 8)
    sweep(v2b, v2a, b2, w2, 0.0625, 6, -3, 7)
    sweep(v2a, v2b, b2, w2, 0.0625, 6, -2, 6)
    prolong(v2b, 6, v1b, 14, -2, 5, 1)
    sweep(v1b, v1a, b1, w1, 0.25, 14, -3, 9)
    sweep(v1a, v1b, b1, w1, 0.25, 14, -2, 8)
    prolong(v1b, 14, v0b, BASE, -2, 7, 0)
    keep = inside(14 + pad, (1, 1, 1, 128), 0)
    v0b[14 + BASE] = v0b[14 + BASE] + jnp.where(keep[0], v1b[7 + 14], 0.0)
    sweep(v0b, v0a, b0, w0, 1.0, BASE, -2, 14)

    def last(start, k, n):
        ext[pl.ds(k + start, n)] = swept(v0a, b0, w0, 1.0, k + (start + BASE), n)

    chunked(0, own + 1, SWEEP_STEP, last)
    keep = pltpu.make_async_copy(ext.at[pl.ds(group * share, share + 1)], pieces.at[group], own_sem)
    keep.start()
    pl.semaphore_wait(barrier, len(everyone))
    sent = []
    passed = []
    half = (share + 1) // 2
    spans = ((0, half), (half, share + 1 - half))
    across = lax.rem(group + 2, CASES)
    for way, (start, many) in enumerate(spans):
        copy = pltpu.make_async_remote_copy(
            src_ref=ext.at[pl.ds(across * share + start, many)],
            dst_ref=relay.at[way, pl.ds(0, many)],
            send_sem=relay_sems.at[0, way],
            recv_sem=relay_sems.at[1, way],
            device_id=(slab, lax.rem(group + (1, CASES - 1)[way], CASES)),
            device_id_type=MESH,
        )
        copy.start()
        sent.append(copy)
    for dx in (1, 3):
        there = lax.rem(group + dx, CASES)
        copy = pltpu.make_async_remote_copy(
            src_ref=ext.at[pl.ds(there * share, share + 1)],
            dst_ref=pieces.at[group],
            send_sem=piece_send.at[there],
            recv_sem=piece_recv.at[group],
            device_id=(slab, there),
            device_id_type=MESH,
        )
        copy.start()
        sent.append(copy)
    for f in range(own):
        for r in range(fields.shape[2]):
            fields[:, f, r, :] = ext[f, r].reshape(cases, 128)

    field_copy = pltpu.make_async_copy(fields, fields_any, field_sem)
    field_copy.start()
    for way, (start, many) in enumerate(spans):
        sent[way].wait_recv()
        source = lax.rem(group + (CASES - 1, 1)[way], CASES)
        copy = pltpu.make_async_remote_copy(
            src_ref=relay.at[way, pl.ds(0, many)],
            dst_ref=pieces.at[source, pl.ds(start, many)],
            send_sem=relay_sems.at[2, way],
            recv_sem=relay_sems.at[3, way],
            device_id=(slab, lax.rem(group + (1, CASES - 1)[way], CASES)),
            device_id_type=MESH,
        )
        copy.start()
        sent.append(copy)
        passed.append(copy)
    every = [
        [pressure[8 * h : 8 * h + 8, 128 * k : 128 * k + 128] for k in range(pressure.shape[1] // 128)]
        for h in range(pressure.shape[0] // 8)
    ]
    for j in range(share):
        p = group * share + (pad + j)
        held = flags[pl.ds(p, 1)].astype(jnp.float32)
        factor = spread((1.0 - held) * span_of(p, held.shape))
        chunk_diag[pl.ds(j, 1)] = spread(diagonal[pl.ds(p, 1)] + 4.0 * held + 6.0)
        loads[pl.ds(j, 1)] = lookup(every, panel[pl.ds(p, 1)]) * factor

    keep.wait()
    for copy in passed:
        copy.wait_recv()
    for dx in (1, 3):
        source = lax.rem(group + dx, CASES)
        pltpu.make_async_remote_copy(
            src_ref=pieces.at[source],
            dst_ref=pieces.at[source],
            send_sem=piece_send.at[source],
            recv_sem=piece_recv.at[source],
            device_id=(slab, source),
            device_id_type=MESH,
        ).wait_recv()

    radial, around = ext.shape[1], ext.shape[-1]
    image_parts, field_parts, above_parts, load_parts = [], [], [], []

    def rows_of(values, r):
        return jnp.concatenate([v[0, r].reshape(-1, around) for v in values], axis=0)

    for j in range(share):
        here = [pieces[g, j : j + 1] for g in range(CASES)]
        above = [pieces[g, j + 1 : j + 2] for g in range(CASES)]
        image = [chunk_diag[j : j + 1] * v - lateral(v) for v in here]
        for r in range(radial):
            image_parts.append(rows_of(image, r))
            field_parts.append(rows_of(here, r))
            above_parts.append(rows_of(above, r))
            load_parts.append(loads[j, r].reshape(-1, around))
    left = jnp.concatenate(
        [jnp.concatenate(parts, axis=1) for parts in (image_parts, above_parts, load_parts)], axis=0
    )
    right = jnp.concatenate(field_parts, axis=1)
    product = lax.dot_general(
        left, right, (((1,), (1,)), ((), ())), precision=highest, preferred_element_type=jnp.float32
    )
    count = right.shape[0]
    coupling = product[count : 2 * count]
    both = jnp.concatenate(
        [product[:count] - (coupling + coupling.T), product[2 * count :]], axis=1
    )
    per = count // CASES
    for g in range(CASES):
        rows[0, g] = both[g * per : (g + 1) * per]
    for dx, dc in mates:
        there_slab, there_group = mate(dx, dc)
        copy = pltpu.make_async_remote_copy(
            src_ref=rows.at[0, there_group],
            dst_ref=rows.at[1 + core, group],
            send_sem=row_send.at[dx, dc],
            recv_sem=row_recv.at[core, group],
            device_id=(there_slab, there_group),
            device_id_type=MESH,
        )
        copy.start()
        sent.append(copy)
    rows[1 + core, group] = rows[0, group]
    for dx, dc in mates:
        source_core, source_group = lax.rem(core + dc, CORES), lax.rem(group + dx, CASES)
        pltpu.make_async_remote_copy(
            src_ref=rows.at[1 + source_core, source_group],
            dst_ref=rows.at[1 + source_core, source_group],
            send_sem=row_send.at[dx, dc],
            recv_sem=row_recv.at[source_core, source_group],
            device_id=(slab, group),
            device_id_type=MESH,
        ).wait_recv()
    total = rows[1, 0]
    for c in range(CORES):
        for g in range(CASES):
            if (c, g) != (0, 0):
                total = total + rows[1 + c, g]

    def combine(total, slots, at, size, device, send, recv):
        slots[at] = total
        for d in range(1, size):
            copy = pltpu.make_async_remote_copy(
                src_ref=slots.at[at],
                dst_ref=slots.at[at],
                send_sem=send.at[d],
                recv_sem=recv.at[at],
                device_id=device(d),
                device_id_type=MESH,
            )
            copy.start()
            sent.append(copy)
        for d in range(1, size):
            source = lax.rem(at + d, size)
            pltpu.make_async_remote_copy(
                src_ref=slots.at[source],
                dst_ref=slots.at[source],
                send_sem=send.at[d],
                recv_sem=recv.at[source],
                device_id=device(d),
                device_id_type=MESH,
            ).wait_recv()
        result = slots[0]
        for d in range(1, size):
            result = result + slots[d]
        return result

    total = combine(total, along_z, z, ZSIZE, z_mate, z_send, z_recv)
    total = combine(total, along_y, y, YSIZE, y_mate, y_send, y_recv)
    gram[...] = total[:, :count]
    cross[...] = total[:, count:]
    for copy in sent:
        copy.wait_send()
    field_copy.wait()


def solve(pressure, panel, flags, diagonal, total, own, radial, around, cases):
    halves = cases // 8
    share = own // CASES
    width = 2 * cases * CASES
    anyspace = pl.BlockSpec(memory_space=pl.ANY)
    vm = pl.BlockSpec(memory_space=pltpu.VMEM)

    def field(n):
        return pltpu.VMEM((n, radial, halves, 8, around), jnp.float32)

    def wide(n):
        return pltpu.VMEM((n, radial, 1, 8, around), jnp.float32)

    def plain(n):
        return pltpu.VMEM((n, radial, around), jnp.float32)

    return pl.pallas_call(
        functools.partial(step_kernel, total),
        out_shape=[
            jax.ShapeDtypeStruct((cases, own, radial, around), jnp.float32),
            jax.ShapeDtypeStruct((cases, width // 2), jnp.float32),
            jax.ShapeDtypeStruct((cases, width // 2), jnp.float32),
        ],
        in_specs=[anyspace] * 4,
        out_specs=[anyspace, vm, vm],
        scratch_shapes=[
            pltpu.VMEM((cases, own, radial, around), jnp.float32),
            pltpu.SemaphoreType.DMA,
            pltpu.VMEM((share, radial, pressure.shape[0] // 8, 8, around), jnp.float32),
            wide(share),
            pltpu.VMEM((CASES, share + 1, radial, halves, 8, around), jnp.float32),
            pltpu.VMEM((1 + CORES, CASES, cases, width), jnp.float32),
            pltpu.VMEM((ZSIZE, cases, width), jnp.float32),
            pltpu.VMEM((YSIZE, cases, width), jnp.float32),
            pltpu.VMEM((2, share + 1 - (share + 1) // 2, radial, halves, 8, around), jnp.float32),
            pltpu.SemaphoreType.DMA((4, 2)),
            pltpu.SemaphoreType.DMA((CASES,)),
            pltpu.SemaphoreType.DMA((CASES,)),
            pltpu.SemaphoreType.DMA((CASES, CORES)),
            pltpu.SemaphoreType.DMA((CORES, CASES)),
            pltpu.SemaphoreType.DMA((ZSIZE,)),
            pltpu.SemaphoreType.DMA((ZSIZE,)),
            pltpu.SemaphoreType.DMA((YSIZE,)),
            pltpu.SemaphoreType.DMA((YSIZE,)),
            pltpu.SemaphoreType.DMA,
            field(own + 1),
            pltpu.VMEM(pressure.shape, jnp.float32),
            pltpu.VMEM(panel.shape, jnp.int32),
            pltpu.VMEM(panel.shape, jnp.int32),
            pltpu.VMEM(panel.shape, jnp.float32),
            pltpu.SemaphoreType.DMA((4,)),
            field(72), plain(72), field(72), field(72), field(72), wide(72), wide(72),
            field(36), plain(36), field(36), field(36), field(36), wide(36), wide(36),
            field(16), field(16), field(16), wide(16),
        ],
        compiler_params=pltpu.CompilerParams(
            collective_id=2, has_side_effects=True, vmem_limit_bytes=64000000
        ),
        name="step",
    )(pressure, panel, flags, diagonal)


def local(pressure, panel, flags, diagonal):
    layers, radial, around = panel.shape
    slabs = lax.axis_size("slab")
    groups = lax.axis_size("case")
    per = pressure.shape[0] // groups
    total = layers * slabs
    spreads = exchange_halo(panel, flags, diagonal, slabs)
    wide = [x.reshape((-1,) + panel.shape[1:]) for x in spreads]
    fields, gram, cross = solve(pressure, *wide, total, layers, radial, around, per)
    scale = 1.0 / (total * radial * around)
    return (fields, gram * scale, cross * scale)


def solution(mesh):
    in_specs = (P(), P("slab", None, None), P("slab", None, None), P("slab", None, None))
    out_specs = (P("case", "slab", None, None), P("case", None), P("case", None))
    return jax.shard_map(local, mesh=mesh, in_specs=in_specs, out_specs=out_specs, check_vma=False)
```

```python
import functools

import jax
import jax.numpy as jnp
from jax import lax
from jax.experimental import pallas as pl
from jax.experimental.pallas import tpu as pltpu
from jax.sharding import PartitionSpec as P

MESH = pl.DeviceIdType.MESH
ZSIZE = 8
YSIZE = 8
CORES = 2
CASES = 4
REACH = 3
BASE = 29
SETUP_STEP = 18
SWEEP_STEP = 36
COARSE_STEP = 11
highest = lax.Precision.HIGHEST


def halo_kernel(slabs, panel, flags, diagonal, panel_out, flags_out, diagonal_out, send, recv, own):
    slab = lax.axis_index("slab")
    barrier = pltpu.get_barrier_semaphore()
    shifts = [d for d in range(-REACH, REACH + 1) if d != 0]
    for d in shifts:
        there = lax.rem(slab + d + slabs, slabs)
        pl.semaphore_signal(barrier, inc=1, device_id={"slab": there}, device_id_type=MESH)
    locals_ = []
    for n, (src, dst) in enumerate(((panel, panel_out), (flags, flags_out), (diagonal, diagonal_out))):
        copy = pltpu.make_async_copy(src, dst.at[REACH], own.at[n])
        copy.start()
        locals_.append(copy)
    pl.semaphore_wait(barrier, len(shifts))
    copies = []
    layers = panel.shape[0]
    for d in sorted(shifts, key=lambda d: -abs(d)):
        there = lax.rem(slab + d + slabs, slabs)
        slot = REACH - d
        start, count = {3: (layers - 5, 5), -3: (0, 6)}.get(d, (0, layers))
        for n, (src, dst) in enumerate(((panel, panel_out), (flags, flags_out), (diagonal, diagonal_out))):
            copy = pltpu.make_async_remote_copy(
                src_ref=src.at[pl.ds(start, count)],
                dst_ref=dst.at[slot, pl.ds(start, count)],
                send_sem=send.at[n, slot],
                recv_sem=recv.at[n, slot],
                device_id={"slab": there},
                device_id_type=MESH,
            )
            copy.start()
            copies.append(copy)
    for copy in locals_:
        copy.wait()
    for copy in copies:
        copy.wait()


def exchange_halo(panel, flags, diagonal, slabs):
    shape = (2 * REACH + 1,) + panel.shape
    anyspace = pl.BlockSpec(memory_space=pl.ANY)
    return pl.pallas_call(
        functools.partial(halo_kernel, slabs),
        out_shape=[
            jax.ShapeDtypeStruct(shape, jnp.int32),
            jax.ShapeDtypeStruct(shape, jnp.int32),
            jax.ShapeDtypeStruct(shape, jnp.float32),
        ],
        in_specs=[anyspace] * 3,
        out_specs=[anyspace] * 3,
        scratch_shapes=[
            pltpu.SemaphoreType.DMA((3, 2 * REACH + 1)),
            pltpu.SemaphoreType.DMA((3, 2 * REACH + 1)),
            pltpu.SemaphoreType.DMA((3,)),
        ],
        compiler_params=pltpu.CompilerParams(collective_id=1, has_side_effects=True),
        name="halo",
    )(panel, flags, diagonal)


def lateral(v):
    flat = v.reshape(-1, v.shape[-1])
    sides = pltpu.roll(flat, 1, 1) + pltpu.roll(flat, flat.shape[1] - 1, 1)
    edge = jnp.zeros_like(v[:, :1])
    inward = jnp.concatenate([edge, v[:, :-1]], axis=1)
    outward = jnp.concatenate([v[:, 1:], edge], axis=1)
    return sides.reshape(v.shape) + (inward + outward)


def spread(row):
    return jnp.broadcast_to(row[:, :, None, None, :], row.shape[:2] + (1, 8, row.shape[2]))


def lookup(blocks, panel_rows):
    layers = []
    for l in range(panel_rows.shape[0]):
        out = []
        for r in range(panel_rows.shape[1]):
            where = jnp.broadcast_to(panel_rows[l, r : r + 1], (8, panel_rows.shape[2]))
            low = where & 127
            high = where >> 7
            hits = [high == j for j in range(1, len(blocks[0]))]
            halves = []
            for pieces in blocks:
                found = jnp.take_along_axis(pieces[0], low, axis=1)
                for j in range(1, len(pieces)):
                    found = jnp.where(hits[j - 1], jnp.take_along_axis(pieces[j], low, axis=1), found)
                halves.append(found)
            out.append(jnp.stack(halves))
        layers.append(jnp.stack(out))
    return jnp.stack(layers)


def chunked(low, high, step, body):
    whole = (high - low) // step

    def run(k, _):
        body(low, step * k, step)
        return 0

    lax.fori_loop(0, whole, run, 0)
    rest = (high - low) - whole * step
    if rest:
        body(low, whole * step, rest)


def step_kernel(total, pressure_any, panel_any, flags_any, diagonal_any, fields_any, gram, cross,
                fields, field_sem, loads, chunk_diag, pieces, rows, along_z, along_y,
                piece_send, piece_recv, row_send, row_recv, z_send, z_recv, y_send, y_recv, own_sem,
                ext, pressure, panel, flags, diagonal, arrive, b0, c0, v0a, v0b, r0, w0, d0, b1, c1, v1a, v1b, r1, w1, d1, b2, v2a, v2b, w2):
    slab = lax.axis_index("slab")
    group = lax.axis_index("case")
    own = fields.shape[1]
    pad = REACH * own
    cases = fields.shape[0]
    core = lax.rem(slab, CORES)
    z = lax.rem(slab // CORES, ZSIZE)
    y = slab // (CORES * ZSIZE)
    pair = slab - core
    share = loads.shape[0]
    barrier = pltpu.get_barrier_semaphore()

    mates = [(dx, dc) for dc in range(CORES) for dx in range(CASES) if (dx, dc) != (0, 0)]

    def mate(dx, dc):
        return (pair + lax.rem(core + dc, CORES), lax.rem(group + dx, CASES))

    def z_mate(d):
        return (y * (ZSIZE * CORES) + lax.rem(z + d, ZSIZE) * CORES + core, group)

    def y_mate(d):
        return (lax.rem(y + d, YSIZE) * (ZSIZE * CORES) + z * CORES + core, group)

    everyone = [mate(dx, dc) for dx, dc in mates]
    everyone += [z_mate(d) for d in range(1, ZSIZE)]
    everyone += [y_mate(d) for d in range(1, YSIZE)]
    for device in everyone:
        pl.semaphore_signal(barrier, inc=1, device_id=device, device_id_type=MESH)
    copies = [
        pltpu.make_async_copy(src, dst, arrive.at[n])
        for n, (src, dst) in enumerate(
            ((pressure_any, pressure), (panel_any, panel), (flags_any, flags), (diagonal_any, diagonal))
        )
    ]
    for copy in copies:
        copy.start()
    for copy in copies:
        copy.wait()
    first = pl.multiple_of(group * cases, cases)
    blocks = [
        [pressure[pl.ds(first + 8 * h, 8), 128 * j : 128 * j + 128] for j in range(pressure.shape[1] // 128)]
        for h in range(cases // 8)
    ]

    def inside(p, shape, level):
        g = lax.broadcasted_iota(jnp.int32, shape, 0) + (p + slab * (own >> level))
        return (g >= pad >> level) & (g < (total + pad) >> level)

    def span_of(p, shape):
        at = (lax.broadcasted_iota(jnp.int32, shape, 0) + (p + slab * own - pad)).astype(jnp.float32)
        return 1.0 + 2.0 * at / total

    def setup(low, k, n):
        p = k + (low + pad - BASE)
        here = pl.ds(k + low, n)
        held = flags[pl.ds(p, n)].astype(jnp.float32)
        coeff = diagonal[pl.ds(p, n)] + 4.0 * held
        c0[here] = coeff
        full = coeff + 6.0
        within = inside(p, full.shape, 0)
        w = spread(jnp.where(within, 0.7 / full, 0.0))
        factor = spread(jnp.where(within, (1.0 - held) * span_of(p, full.shape), 0.0))
        w0[here] = w
        d0[here] = spread(full)
        rhs = lookup(blocks, panel[pl.ds(p, n)]) * factor
        b0[here] = rhs
        v0a[here] = w * rhs

    chunked(0, 71, SETUP_STEP, setup)

    def swept(src, rhs, w, weight, at, n):
        wide = src[pl.ds(at - 1, n + 2)]
        v = wide[1:-1]
        near = wide[:-2] + wide[2:]
        if weight != 1.0:
            near = weight * near
        return 0.3 * v + w[pl.ds(at, n)] * (rhs[pl.ds(at, n)] + near + lateral(v))

    def sweep(src, dst, rhs, w, weight, base, low, high):
        def body(start, k, n):
            dst[pl.ds(k + start, n)] = swept(src, rhs, w, weight, k + start, n)

        chunked(low + base, high + base, SWEEP_STEP, body)

    def residual(src, dst, rhs, full, weight, base, low, high, level):
        def body(start, k, n):
            at = k + start
            wide = src[pl.ds(at - 1, n + 2)]
            v = wide[1:-1]
            near = wide[:-2] + wide[2:]
            if weight != 1.0:
                near = weight * near
            left = rhs[pl.ds(at, n)] - full[pl.ds(at, n)] * v + (near + lateral(v))
            for j in range(n):
                keep = inside(at + ((pad >> level) - base) + j, (1, 1, 1, 128), level)
                dst[at + j] = jnp.where(keep, left[j], 0.0)

        chunked(low + base, high + base, SWEEP_STEP, body)

    def restrict(fine, fine_base, cfine, rhs, ccoarse, w, full, vinit, weight, base, low, high, level):
        def body(start, k, n):
            for j in range(n):
                at = 2 * k + (fine_base + 2 * low + 2 * j)
                i = k + (start + j)
                value = 0.5 * fine[at] + 0.25 * (fine[at + 1] + fine[at - 1])
                coeff = 0.5 * (cfine[at] + cfine[at + 1])
                diag = coeff + (2.0 * weight + 4.0)
                if ccoarse is not None:
                    ccoarse[i] = coeff
                    full[i] = spread(diag[None])[0]
                keep = inside(k + (low + (pad >> level) + j), (1, 128), level)
                scale = spread(jnp.where(keep, 0.7 / diag, 0.0)[None])[0]
                w[i] = scale
                rhs[i] = value
                vinit[i] = scale * value

        chunked(low + base, high + base, COARSE_STEP, body)

    def prolong(coarse, coarse_base, v, base, low, high, level):
        def body(start, k, n):
            wide = coarse[pl.ds(k + start, n + 1)]
            between = 0.5 * (wide[:-1] + wide[1:])
            for j in range(n):
                at = 2 * k + (2 * low + base + 2 * j)
                p = 2 * k + (2 * low + (pad >> level) + 2 * j)
                keep = inside(p, (1, 1, 1, 128), level)
                v[at] = v[at] + jnp.where(keep, wide[j], 0.0)
                keep = inside(p + 1, (1, 1, 1, 128), level)
                v[at + 1] = v[at + 1] + jnp.where(keep, between[j], 0.0)

        chunked(low + coarse_base, high + coarse_base, COARSE_STEP, body)

    sweep(v0a, v0b, b0, w0, 1.0, BASE, -28, 41)
    residual(v0b, r0, b0, d0, 1.0, BASE, -27, 40, 0)
    restrict(r0, BASE, c0, b1, c1, w1, d1, v1a, 0.25, 14, -13, 20, 1)
    sweep(v1a, v1b, b1, w1, 0.25, 14, -12, 19)
    residual(v1b, r1, b1, d1, 0.25, 14, -11, 18, 1)
    restrict(r1, 14, c1, b2, None, w2, None, v2a, 0.0625, 6, -5, 9, 2)
    sweep(v2a, v2b, b2, w2, 0.0625, 6, -4, 8)
    sweep(v2b, v2a, b2, w2, 0.0625, 6, -3, 7)
    sweep(v2a, v2b, b2, w2, 0.0625, 6, -2, 6)
    prolong(v2b, 6, v1b, 14, -2, 5, 1)
    sweep(v1b, v1a, b1, w1, 0.25, 14, -3, 9)
    sweep(v1a, v1b, b1, w1, 0.25, 14, -2, 8)
    prolong(v1b, 14, v0b, BASE, -2, 7, 0)
    keep = inside(14 + pad, (1, 1, 1, 128), 0)
    v0b[14 + BASE] = v0b[14 + BASE] + jnp.where(keep[0], v1b[7 + 14], 0.0)
    sweep(v0b, v0a, b0, w0, 1.0, BASE, -2, 14)

    def last(start, k, n):
        ext[pl.ds(k + start, n)] = swept(v0a, b0, w0, 1.0, k + (start + BASE), n)

    chunked(0, own + 1, SWEEP_STEP, last)
    keep = pltpu.make_async_copy(ext.at[pl.ds(group * share, share + 1)], pieces.at[group], own_sem)
    keep.start()
    pl.semaphore_wait(barrier, len(everyone))
    sent = []
    for dx in (2, 1, 3):
        there = lax.rem(group + dx, CASES)
        copy = pltpu.make_async_remote_copy(
            src_ref=ext.at[pl.ds(there * share, share + 1)],
            dst_ref=pieces.at[group],
            send_sem=piece_send.at[there],
            recv_sem=piece_recv.at[group],
            device_id=(slab, there),
            device_id_type=MESH,
        )
        copy.start()
        sent.append(copy)
    for f in range(own):
        for r in range(fields.shape[2]):
            fields[:, f, r, :] = ext[f, r].reshape(cases, 128)

    field_copy = pltpu.make_async_copy(fields, fields_any, field_sem)
    field_copy.start()
    every = [
        [pressure[8 * h : 8 * h + 8, 128 * k : 128 * k + 128] for k in range(pressure.shape[1] // 128)]
        for h in range(pressure.shape[0] // 8)
    ]
    for j in range(share):
        p = group * share + (pad + j)
        held = flags[pl.ds(p, 1)].astype(jnp.float32)
        factor = spread((1.0 - held) * span_of(p, held.shape))
        chunk_diag[pl.ds(j, 1)] = spread(diagonal[pl.ds(p, 1)] + 4.0 * held + 6.0)
        loads[pl.ds(j, 1)] = lookup(every, panel[pl.ds(p, 1)]) * factor

    keep.wait()
    for dx in (1, 2, 3):
        source = lax.rem(group + dx, CASES)
        pltpu.make_async_remote_copy(
            src_ref=pieces.at[source],
            dst_ref=pieces.at[source],
            send_sem=piece_send.at[source],
            recv_sem=piece_recv.at[source],
            device_id=(slab, source),
            device_id_type=MESH,
        ).wait_recv()

    radial, around = ext.shape[1], ext.shape[-1]
    image_parts, field_parts, above_parts, load_parts = [], [], [], []

    def rows_of(values, r):
        return jnp.concatenate([v[0, r].reshape(-1, around) for v in values], axis=0)

    for j in range(share):
        here = [pieces[g, j : j + 1] for g in range(CASES)]
        above = [pieces[g, j + 1 : j + 2] for g in range(CASES)]
        image = [chunk_diag[j : j + 1] * v - lateral(v) for v in here]
        for r in range(radial):
            image_parts.append(rows_of(image, r))
            field_parts.append(rows_of(here, r))
            above_parts.append(rows_of(above, r))
            load_parts.append(loads[j, r].reshape(-1, around))
    left = jnp.concatenate(
        [jnp.concatenate(parts, axis=1) for parts in (image_parts, above_parts, load_parts)], axis=0
    )
    right = jnp.concatenate(field_parts, axis=1)
    product = lax.dot_general(
        left, right, (((1,), (1,)), ((), ())), precision=highest, preferred_element_type=jnp.float32
    )
    count = right.shape[0]
    coupling = product[count : 2 * count]
    both = jnp.concatenate(
        [product[:count] - (coupling + coupling.T), product[2 * count :]], axis=1
    )
    per = count // CASES
    for g in range(CASES):
        rows[0, g] = both[g * per : (g + 1) * per]
    for dx, dc in mates:
        there_slab, there_group = mate(dx, dc)
        copy = pltpu.make_async_remote_copy(
            src_ref=rows.at[0, there_group],
            dst_ref=rows.at[1 + core, group],
            send_sem=row_send.at[dx, dc],
            recv_sem=row_recv.at[core, group],
            device_id=(there_slab, there_group),
            device_id_type=MESH,
        )
        copy.start()
        sent.append(copy)
    rows[1 + core, group] = rows[0, group]
    for dx, dc in mates:
        source_core, source_group = lax.rem(core + dc, CORES), lax.rem(group + dx, CASES)
        pltpu.make_async_remote_copy(
            src_ref=rows.at[1 + source_core, source_group],
            dst_ref=rows.at[1 + source_core, source_group],
            send_sem=row_send.at[dx, dc],
            recv_sem=row_recv.at[source_core, source_group],
            device_id=(slab, group),
            device_id_type=MESH,
        ).wait_recv()
    total_rows = rows[1, 0]
    for c in range(CORES):
        for g in range(CASES):
            if (c, g) != (0, 0):
                total_rows = total_rows + rows[1 + c, g]

    def spread_out(value, slots, at, size, device, send, recv):
        slots[at] = value
        for d in range(1, size):
            copy = pltpu.make_async_remote_copy(
                src_ref=slots.at[at],
                dst_ref=slots.at[at],
                send_sem=send.at[d],
                recv_sem=recv.at[at],
                device_id=device(d),
                device_id_type=MESH,
            )
            copy.start()
            sent.append(copy)

    def add_up(slots, at, size, device, send, recv):
        for d in range(1, size):
            source = lax.rem(at + d, size)
            pltpu.make_async_remote_copy(
                src_ref=slots.at[source],
                dst_ref=slots.at[source],
                send_sem=send.at[d],
                recv_sem=recv.at[source],
                device_id=device(d),
                device_id_type=MESH,
            ).wait_recv()
        result = slots[0]
        for d in range(1, size):
            result = result + slots[d]
        return result

    half = total_rows.shape[0] // 2
    z_way = [(along_z.at[n], z, ZSIZE, z_mate, z_send.at[n], z_recv.at[n]) for n in range(2)]
    y_way = [(along_y.at[n], y, YSIZE, y_mate, y_send.at[n], y_recv.at[n]) for n in range(2)]
    spread_out(total_rows[:half], *z_way[0])
    spread_out(total_rows[half:], *y_way[1])
    upper = add_up(*z_way[0])
    spread_out(upper, *y_way[0])
    lower = add_up(*y_way[1])
    spread_out(lower, *z_way[1])
    upper = add_up(*y_way[0])
    lower = add_up(*z_way[1])
    gram[:half] = upper[:, :count]
    gram[half:] = lower[:, :count]
    cross[:half] = upper[:, count:]
    cross[half:] = lower[:, count:]
    for copy in sent:
        copy.wait_send()
    field_copy.wait()


def solve(pressure, panel, flags, diagonal, total, own, radial, around, cases):
    halves = cases // 8
    share = own // CASES
    width = 2 * cases * CASES
    anyspace = pl.BlockSpec(memory_space=pl.ANY)
    vm = pl.BlockSpec(memory_space=pltpu.VMEM)

    def field(n):
        return pltpu.VMEM((n, radial, halves, 8, around), jnp.float32)

    def wide(n):
        return pltpu.VMEM((n, radial, 1, 8, around), jnp.float32)

    def plain(n):
        return pltpu.VMEM((n, radial, around), jnp.float32)

    return pl.pallas_call(
        functools.partial(step_kernel, total),
        out_shape=[
            jax.ShapeDtypeStruct((cases, own, radial, around), jnp.float32),
            jax.ShapeDtypeStruct((cases, width // 2), jnp.float32),
            jax.ShapeDtypeStruct((cases, width // 2), jnp.float32),
        ],
        in_specs=[anyspace] * 4,
        out_specs=[anyspace, vm, vm],
        scratch_shapes=[
            pltpu.VMEM((cases, own, radial, around), jnp.float32),
            pltpu.SemaphoreType.DMA,
            pltpu.VMEM((share, radial, pressure.shape[0] // 8, 8, around), jnp.float32),
            wide(share),
            pltpu.VMEM((CASES, share + 1, radial, halves, 8, around), jnp.float32),
            pltpu.VMEM((1 + CORES, CASES, cases, width), jnp.float32),
            pltpu.VMEM((2, ZSIZE, cases // 2, width), jnp.float32),
            pltpu.VMEM((2, YSIZE, cases // 2, width), jnp.float32),
            pltpu.SemaphoreType.DMA((CASES,)),
            pltpu.SemaphoreType.DMA((CASES,)),
            pltpu.SemaphoreType.DMA((CASES, CORES)),
            pltpu.SemaphoreType.DMA((CORES, CASES)),
            pltpu.SemaphoreType.DMA((2, ZSIZE)),
            pltpu.SemaphoreType.DMA((2, ZSIZE)),
            pltpu.SemaphoreType.DMA((2, YSIZE)),
            pltpu.SemaphoreType.DMA((2, YSIZE)),
            pltpu.SemaphoreType.DMA,
            field(own + 1),
            pltpu.VMEM(pressure.shape, jnp.float32),
            pltpu.VMEM(panel.shape, jnp.int32),
            pltpu.VMEM(panel.shape, jnp.int32),
            pltpu.VMEM(panel.shape, jnp.float32),
            pltpu.SemaphoreType.DMA((4,)),
            field(72), plain(72), field(72), field(72), field(72), wide(72), wide(72),
            field(36), plain(36), field(36), field(36), field(36), wide(36), wide(36),
            field(16), field(16), field(16), wide(16),
        ],
        compiler_params=pltpu.CompilerParams(
            collective_id=2, has_side_effects=True, vmem_limit_bytes=64000000
        ),
        name="step",
    )(pressure, panel, flags, diagonal)


def local(pressure, panel, flags, diagonal):
    layers, radial, around = panel.shape
    slabs = lax.axis_size("slab")
    groups = lax.axis_size("case")
    per = pressure.shape[0] // groups
    total = layers * slabs
    spreads = exchange_halo(panel, flags, diagonal, slabs)
    wide = [x.reshape((-1,) + panel.shape[1:]) for x in spreads]
    fields, gram, cross = solve(pressure, *wide, total, layers, radial, around, per)
    scale = 1.0 / (total * radial * around)
    return (fields, gram * scale, cross * scale)


def solution(mesh):
    in_specs = (P(), P("slab", None, None), P("slab", None, None), P("slab", None, None))
    out_specs = (P("case", "slab", None, None), P("case", None), P("case", None))
    return jax.shard_map(local, mesh=mesh, in_specs=in_specs, out_specs=out_specs, check_vma=False)
```

```python
import functools

import jax
import jax.numpy as jnp
from jax import lax
from jax.experimental import pallas as pl
from jax.experimental.pallas import tpu as pltpu
from jax.sharding import PartitionSpec as P

MESH = pl.DeviceIdType.MESH
ZSIZE = 8
YSIZE = 8
CORES = 2
CASES = 4
REACH = 3
BASE = 29
SETUP_STEP = 18
SWEEP_STEP = 36
COARSE_STEP = 33
highest = lax.Precision.HIGHEST


def halo_kernel(slabs, panel, flags, diagonal, panel_out, flags_out, diagonal_out, send, recv, own):
    slab = lax.axis_index("slab")
    barrier = pltpu.get_barrier_semaphore()
    shifts = [d for d in range(-REACH, REACH + 1) if d != 0]
    for d in shifts:
        there = lax.rem(slab + d + slabs, slabs)
        pl.semaphore_signal(barrier, inc=1, device_id={"slab": there}, device_id_type=MESH)
    locals_ = []
    for n, (src, dst) in enumerate(((panel, panel_out), (flags, flags_out), (diagonal, diagonal_out))):
        copy = pltpu.make_async_copy(src, dst.at[REACH], own.at[n])
        copy.start()
        locals_.append(copy)
    pl.semaphore_wait(barrier, len(shifts))
    copies = []
    layers = panel.shape[0]
    for d in sorted(shifts, key=lambda d: -abs(d)):
        there = lax.rem(slab + d + slabs, slabs)
        slot = REACH - d
        start, count = {3: (layers - 5, 5), -3: (0, 6)}.get(d, (0, layers))
        for n, (src, dst) in enumerate(((panel, panel_out), (flags, flags_out), (diagonal, diagonal_out))):
            copy = pltpu.make_async_remote_copy(
                src_ref=src.at[pl.ds(start, count)],
                dst_ref=dst.at[slot, pl.ds(start, count)],
                send_sem=send.at[n, slot],
                recv_sem=recv.at[n, slot],
                device_id={"slab": there},
                device_id_type=MESH,
            )
            copy.start()
            copies.append(copy)
    for copy in locals_:
        copy.wait()
    for copy in copies:
        copy.wait()


def exchange_halo(panel, flags, diagonal, slabs):
    shape = (2 * REACH + 1,) + panel.shape
    anyspace = pl.BlockSpec(memory_space=pl.ANY)
    return pl.pallas_call(
        functools.partial(halo_kernel, slabs),
        out_shape=[
            jax.ShapeDtypeStruct(shape, jnp.int32),
            jax.ShapeDtypeStruct(shape, jnp.int32),
            jax.ShapeDtypeStruct(shape, jnp.float32),
        ],
        in_specs=[anyspace] * 3,
        out_specs=[anyspace] * 3,
        scratch_shapes=[
            pltpu.SemaphoreType.DMA((3, 2 * REACH + 1)),
            pltpu.SemaphoreType.DMA((3, 2 * REACH + 1)),
            pltpu.SemaphoreType.DMA((3,)),
        ],
        compiler_params=pltpu.CompilerParams(collective_id=1, has_side_effects=True),
        name="halo",
    )(panel, flags, diagonal)


def lateral(v):
    flat = v.reshape(-1, v.shape[-1])
    sides = pltpu.roll(flat, 1, 1) + pltpu.roll(flat, flat.shape[1] - 1, 1)
    edge = jnp.zeros_like(v[:, :1])
    inward = jnp.concatenate([edge, v[:, :-1]], axis=1)
    outward = jnp.concatenate([v[:, 1:], edge], axis=1)
    return sides.reshape(v.shape) + (inward + outward)


def spread(row):
    return jnp.broadcast_to(row[:, :, None, None, :], row.shape[:2] + (1, 8, row.shape[2]))


def lookup(blocks, panel_rows):
    layers = []
    for l in range(panel_rows.shape[0]):
        out = []
        for r in range(panel_rows.shape[1]):
            where = jnp.broadcast_to(panel_rows[l, r : r + 1], (8, panel_rows.shape[2]))
            low = where & 127
            high = where >> 7
            hits = [high == j for j in range(1, len(blocks[0]))]
            halves = []
            for pieces in blocks:
                found = jnp.take_along_axis(pieces[0], low, axis=1)
                for j in range(1, len(pieces)):
                    found = jnp.where(hits[j - 1], jnp.take_along_axis(pieces[j], low, axis=1), found)
                halves.append(found)
            out.append(jnp.stack(halves))
        layers.append(jnp.stack(out))
    return jnp.stack(layers)


def chunked(low, high, step, body):
    whole = (high - low) // step

    def run(k, _):
        body(low, step * k, step)
        return 0

    lax.fori_loop(0, whole, run, 0)
    rest = (high - low) - whole * step
    if rest:
        body(low, whole * step, rest)


def step_kernel(total, pressure_any, panel_any, flags_any, diagonal_any, fields_any, gram, cross,
                fields, field_sem, loads, chunk_diag, pieces, rows, along_z, along_y,
                piece_send, piece_recv, row_send, row_recv, z_send, z_recv, y_send, y_recv, own_sem,
                ext, pressure, panel, flags, diagonal, arrive, b0, c0, v0a, v0b, r0, w0, d0, b1, c1, v1a, v1b, r1, w1, d1, b2, v2a, v2b, w2):
    slab = lax.axis_index("slab")
    group = lax.axis_index("case")
    own = fields.shape[1]
    pad = REACH * own
    cases = fields.shape[0]
    core = lax.rem(slab, CORES)
    z = lax.rem(slab // CORES, ZSIZE)
    y = slab // (CORES * ZSIZE)
    pair = slab - core
    share = loads.shape[0]
    barrier = pltpu.get_barrier_semaphore()

    mates = [(dx, dc) for dc in range(CORES) for dx in range(CASES) if (dx, dc) != (0, 0)]

    def mate(dx, dc):
        return (pair + lax.rem(core + dc, CORES), lax.rem(group + dx, CASES))

    def z_mate(d):
        return (y * (ZSIZE * CORES) + lax.rem(z + d, ZSIZE) * CORES + core, group)

    def y_mate(d):
        return (lax.rem(y + d, YSIZE) * (ZSIZE * CORES) + z * CORES + core, group)

    everyone = [mate(dx, dc) for dx, dc in mates]
    everyone += [z_mate(d) for d in range(1, ZSIZE)]
    everyone += [y_mate(d) for d in range(1, YSIZE)]
    for device in everyone:
        pl.semaphore_signal(barrier, inc=1, device_id=device, device_id_type=MESH)
    copies = [
        pltpu.make_async_copy(src, dst, arrive.at[n])
        for n, (src, dst) in enumerate(
            ((pressure_any, pressure), (panel_any, panel), (flags_any, flags), (diagonal_any, diagonal))
        )
    ]
    for copy in copies:
        copy.start()
    for copy in copies:
        copy.wait()
    first = pl.multiple_of(group * cases, cases)
    blocks = [
        [pressure[pl.ds(first + 8 * h, 8), 128 * j : 128 * j + 128] for j in range(pressure.shape[1] // 128)]
        for h in range(cases // 8)
    ]

    def inside(p, shape, level):
        g = lax.broadcasted_iota(jnp.int32, shape, 0) + (p + slab * (own >> level))
        return (g >= pad >> level) & (g < (total + pad) >> level)

    def span_of(p, shape):
        at = (lax.broadcasted_iota(jnp.int32, shape, 0) + (p + slab * own - pad)).astype(jnp.float32)
        return 1.0 + 2.0 * at / total

    def setup(low, k, n):
        p = k + (low + pad - BASE)
        here = pl.ds(k + low, n)
        held = flags[pl.ds(p, n)].astype(jnp.float32)
        coeff = diagonal[pl.ds(p, n)] + 4.0 * held
        c0[here] = coeff
        full = coeff + 6.0
        within = inside(p, full.shape, 0)
        w = spread(jnp.where(within, 0.7 / full, 0.0))
        factor = spread(jnp.where(within, (1.0 - held) * span_of(p, full.shape), 0.0))
        w0[here] = w
        d0[here] = spread(full)
        rhs = lookup(blocks, panel[pl.ds(p, n)]) * factor
        b0[here] = rhs
        v0a[here] = w * rhs

    chunked(0, 71, SETUP_STEP, setup)

    def swept(src, rhs, w, weight, at, n):
        wide = src[pl.ds(at - 1, n + 2)]
        v = wide[1:-1]
        near = wide[:-2] + wide[2:]
        if weight != 1.0:
            near = weight * near
        return 0.3 * v + w[pl.ds(at, n)] * (rhs[pl.ds(at, n)] + near + lateral(v))

    def sweep(src, dst, rhs, w, weight, base, low, high):
        def body(start, k, n):
            dst[pl.ds(k + start, n)] = swept(src, rhs, w, weight, k + start, n)

        chunked(low + base, high + base, SWEEP_STEP, body)

    def residual(src, dst, rhs, full, weight, base, low, high, level):
        def body(start, k, n):
            at = k + start
            wide = src[pl.ds(at - 1, n + 2)]
            v = wide[1:-1]
            near = wide[:-2] + wide[2:]
            if weight != 1.0:
                near = weight * near
            left = rhs[pl.ds(at, n)] - full[pl.ds(at, n)] * v + (near + lateral(v))
            for j in range(n):
                keep = inside(at + ((pad >> level) - base) + j, (1, 1, 1, 128), level)
                dst[at + j] = jnp.where(keep, left[j], 0.0)

        chunked(low + base, high + base, SWEEP_STEP, body)

    def restrict(fine, fine_base, cfine, rhs, ccoarse, w, full, vinit, weight, base, low, high, level):
        def body(start, k, n):
            for j in range(n):
                at = 2 * k + (fine_base + 2 * low + 2 * j)
                i = k + (start + j)
                value = 0.5 * fine[at] + 0.25 * (fine[at + 1] + fine[at - 1])
                coeff = 0.5 * (cfine[at] + cfine[at + 1])
                diag = coeff + (2.0 * weight + 4.0)
                if ccoarse is not None:
                    ccoarse[i] = coeff
                    full[i] = spread(diag[None])[0]
                keep = inside(k + (low + (pad >> level) + j), (1, 128), level)
                scale = spread(jnp.where(keep, 0.7 / diag, 0.0)[None])[0]
                w[i] = scale
                rhs[i] = value
                vinit[i] = scale * value

        chunked(low + base, high + base, COARSE_STEP, body)

    def prolong(coarse, coarse_base, v, base, low, high, level):
        def body(start, k, n):
            wide = coarse[pl.ds(k + start, n + 1)]
            between = 0.5 * (wide[:-1] + wide[1:])
            for j in range(n):
                at = 2 * k + (2 * low + base + 2 * j)
                p = 2 * k + (2 * low + (pad >> level) + 2 * j)
                keep = inside(p, (1, 1, 1, 128), level)
                v[at] = v[at] + jnp.where(keep, wide[j], 0.0)
                keep = inside(p + 1, (1, 1, 1, 128), level)
                v[at + 1] = v[at + 1] + jnp.where(keep, between[j], 0.0)

        chunked(low + coarse_base, high + coarse_base, COARSE_STEP, body)

    sweep(v0a, v0b, b0, w0, 1.0, BASE, -28, 41)
    residual(v0b, r0, b0, d0, 1.0, BASE, -27, 40, 0)
    restrict(r0, BASE, c0, b1, c1, w1, d1, v1a, 0.25, 14, -13, 20, 1)
    sweep(v1a, v1b, b1, w1, 0.25, 14, -12, 19)
    residual(v1b, r1, b1, d1, 0.25, 14, -11, 18, 1)
    restrict(r1, 14, c1, b2, None, w2, None, v2a, 0.0625, 6, -5, 9, 2)
    sweep(v2a, v2b, b2, w2, 0.0625, 6, -4, 8)
    sweep(v2b, v2a, b2, w2, 0.0625, 6, -3, 7)
    sweep(v2a, v2b, b2, w2, 0.0625, 6, -2, 6)
    prolong(v2b, 6, v1b, 14, -2, 5, 1)
    sweep(v1b, v1a, b1, w1, 0.25, 14, -3, 9)
    sweep(v1a, v1b, b1, w1, 0.25, 14, -2, 8)
    prolong(v1b, 14, v0b, BASE, -2, 7, 0)
    keep = inside(14 + pad, (1, 1, 1, 128), 0)
    v0b[14 + BASE] = v0b[14 + BASE] + jnp.where(keep[0], v1b[7 + 14], 0.0)
    sweep(v0b, v0a, b0, w0, 1.0, BASE, -2, 14)

    def last(start, k, n):
        ext[pl.ds(k + start, n)] = swept(v0a, b0, w0, 1.0, k + (start + BASE), n)

    chunked(0, own + 1, SWEEP_STEP, last)
    keep = pltpu.make_async_copy(ext.at[pl.ds(group * share, share + 1)], pieces.at[group], own_sem)
    keep.start()
    pl.semaphore_wait(barrier, len(everyone))
    sent = []
    for dx in (2, 1, 3):
        there = lax.rem(group + dx, CASES)
        copy = pltpu.make_async_remote_copy(
            src_ref=ext.at[pl.ds(there * share, share + 1)],
            dst_ref=pieces.at[group],
            send_sem=piece_send.at[there],
            recv_sem=piece_recv.at[group],
            device_id=(slab, there),
            device_id_type=MESH,
        )
        copy.start()
        sent.append(copy)
    for f in range(own):
        for r in range(fields.shape[2]):
            fields[:, f, r, :] = ext[f, r].reshape(cases, 128)

    field_copy = pltpu.make_async_copy(fields, fields_any, field_sem)
    field_copy.start()
    every = [
        [pressure[8 * h : 8 * h + 8, 128 * k : 128 * k + 128] for k in range(pressure.shape[1] // 128)]
        for h in range(pressure.shape[0] // 8)
    ]
    for j in range(share):
        p = group * share + (pad + j)
        held = flags[pl.ds(p, 1)].astype(jnp.float32)
        factor = spread((1.0 - held) * span_of(p, held.shape))
        chunk_diag[pl.ds(j, 1)] = spread(diagonal[pl.ds(p, 1)] + 4.0 * held + 6.0)
        loads[pl.ds(j, 1)] = lookup(every, panel[pl.ds(p, 1)]) * factor

    keep.wait()
    for dx in (1, 2, 3):
        source = lax.rem(group + dx, CASES)
        pltpu.make_async_remote_copy(
            src_ref=pieces.at[source],
            dst_ref=pieces.at[source],
            send_sem=piece_send.at[source],
            recv_sem=piece_recv.at[source],
            device_id=(slab, source),
            device_id_type=MESH,
        ).wait_recv()

    radial, around = ext.shape[1], ext.shape[-1]
    image_parts, field_parts, above_parts, load_parts = [], [], [], []

    def rows_of(values, r):
        return jnp.concatenate([v[0, r].reshape(-1, around) for v in values], axis=0)

    for j in range(share):
        here = [pieces[g, j : j + 1] for g in range(CASES)]
        above = [pieces[g, j + 1 : j + 2] for g in range(CASES)]
        image = [chunk_diag[j : j + 1] * v - lateral(v) for v in here]
        for r in range(radial):
            image_parts.append(rows_of(image, r))
            field_parts.append(rows_of(here, r))
            above_parts.append(rows_of(above, r))
            load_parts.append(loads[j, r].reshape(-1, around))
    left = jnp.concatenate(
        [jnp.concatenate(parts, axis=1) for parts in (image_parts, above_parts, load_parts)], axis=0
    )
    right = jnp.concatenate(field_parts, axis=1)
    product = lax.dot_general(
        left, right, (((1,), (1,)), ((), ())), precision=highest, preferred_element_type=jnp.float32
    )
    count = right.shape[0]
    coupling = product[count : 2 * count]
    both = jnp.concatenate(
        [product[:count] - (coupling + coupling.T), product[2 * count :]], axis=1
    )
    per = count // CASES
    for g in range(CASES):
        rows[0, g] = both[g * per : (g + 1) * per]
    for dx, dc in mates:
        there_slab, there_group = mate(dx, dc)
        copy = pltpu.make_async_remote_copy(
            src_ref=rows.at[0, there_group],
            dst_ref=rows.at[1 + core, group],
            send_sem=row_send.at[dx, dc],
            recv_sem=row_recv.at[core, group],
            device_id=(there_slab, there_group),
            device_id_type=MESH,
        )
        copy.start()
        sent.append(copy)
    rows[1 + core, group] = rows[0, group]
    for dx, dc in mates:
        source_core, source_group = lax.rem(core + dc, CORES), lax.rem(group + dx, CASES)
        pltpu.make_async_remote_copy(
            src_ref=rows.at[1 + source_core, source_group],
            dst_ref=rows.at[1 + source_core, source_group],
            send_sem=row_send.at[dx, dc],
            recv_sem=row_recv.at[source_core, source_group],
            device_id=(slab, group),
            device_id_type=MESH,
        ).wait_recv()
    total_rows = rows[1, 0]
    for c in range(CORES):
        for g in range(CASES):
            if (c, g) != (0, 0):
                total_rows = total_rows + rows[1 + c, g]

    def spread_out(value, slots, at, size, device, send, recv):
        slots[at] = value
        for d in range(1, size):
            copy = pltpu.make_async_remote_copy(
                src_ref=slots.at[at],
                dst_ref=slots.at[at],
                send_sem=send.at[d],
                recv_sem=recv.at[at],
                device_id=device(d),
                device_id_type=MESH,
            )
            copy.start()
            sent.append(copy)

    def add_up(slots, at, size, device, send, recv):
        for d in range(1, size):
            source = lax.rem(at + d, size)
            pltpu.make_async_remote_copy(
                src_ref=slots.at[source],
                dst_ref=slots.at[source],
                send_sem=send.at[d],
                recv_sem=recv.at[source],
                device_id=device(d),
                device_id_type=MESH,
            ).wait_recv()
        result = slots[0]
        for d in range(1, size):
            result = result + slots[d]
        return result

    half = total_rows.shape[0] // 2
    z_way = [(along_z.at[n], z, ZSIZE, z_mate, z_send.at[n], z_recv.at[n]) for n in range(2)]
    y_way = [(along_y.at[n], y, YSIZE, y_mate, y_send.at[n], y_recv.at[n]) for n in range(2)]
    spread_out(total_rows[:half], *z_way[0])
    spread_out(total_rows[half:], *y_way[1])
    upper = add_up(*z_way[0])
    spread_out(upper, *y_way[0])
    lower = add_up(*y_way[1])
    spread_out(lower, *z_way[1])
    upper = add_up(*y_way[0])
    lower = add_up(*z_way[1])
    gram[:half] = upper[:, :count]
    gram[half:] = lower[:, :count]
    cross[:half] = upper[:, count:]
    cross[half:] = lower[:, count:]
    for copy in sent:
        copy.wait_send()
    field_copy.wait()


def solve(pressure, panel, flags, diagonal, total, own, radial, around, cases):
    halves = cases // 8
    share = own // CASES
    width = 2 * cases * CASES
    anyspace = pl.BlockSpec(memory_space=pl.ANY)
    vm = pl.BlockSpec(memory_space=pltpu.VMEM)

    def field(n):
        return pltpu.VMEM((n, radial, halves, 8, around), jnp.float32)

    def wide(n):
        return pltpu.VMEM((n, radial, 1, 8, around), jnp.float32)

    def plain(n):
        return pltpu.VMEM((n, radial, around), jnp.float32)

    return pl.pallas_call(
        functools.partial(step_kernel, total),
        out_shape=[
            jax.ShapeDtypeStruct((cases, own, radial, around), jnp.float32),
            jax.ShapeDtypeStruct((cases, width // 2), jnp.float32),
            jax.ShapeDtypeStruct((cases, width // 2), jnp.float32),
        ],
        in_specs=[anyspace] * 4,
        out_specs=[anyspace, vm, vm],
        scratch_shapes=[
            pltpu.VMEM((cases, own, radial, around), jnp.float32),
            pltpu.SemaphoreType.DMA,
            pltpu.VMEM((share, radial, pressure.shape[0] // 8, 8, around), jnp.float32),
            wide(share),
            pltpu.VMEM((CASES, share + 1, radial, halves, 8, around), jnp.float32),
            pltpu.VMEM((1 + CORES, CASES, cases, width), jnp.float32),
            pltpu.VMEM((2, ZSIZE, cases // 2, width), jnp.float32),
            pltpu.VMEM((2, YSIZE, cases // 2, width), jnp.float32),
            pltpu.SemaphoreType.DMA((CASES,)),
            pltpu.SemaphoreType.DMA((CASES,)),
            pltpu.SemaphoreType.DMA((CASES, CORES)),
            pltpu.SemaphoreType.DMA((CORES, CASES)),
            pltpu.SemaphoreType.DMA((2, ZSIZE)),
            pltpu.SemaphoreType.DMA((2, ZSIZE)),
            pltpu.SemaphoreType.DMA((2, YSIZE)),
            pltpu.SemaphoreType.DMA((2, YSIZE)),
            pltpu.SemaphoreType.DMA,
            field(own + 1),
            pltpu.VMEM(pressure.shape, jnp.float32),
            pltpu.VMEM(panel.shape, jnp.int32),
            pltpu.VMEM(panel.shape, jnp.int32),
            pltpu.VMEM(panel.shape, jnp.float32),
            pltpu.SemaphoreType.DMA((4,)),
            field(72), plain(72), field(72), field(72), field(72), wide(72), wide(72),
            field(36), plain(36), field(36), field(36), field(36), wide(36), wide(36),
            field(16), field(16), field(16), wide(16),
        ],
        compiler_params=pltpu.CompilerParams(
            collective_id=2, has_side_effects=True, vmem_limit_bytes=64000000
        ),
        name="step",
    )(pressure, panel, flags, diagonal)


def local(pressure, panel, flags, diagonal):
    layers, radial, around = panel.shape
    slabs = lax.axis_size("slab")
    groups = lax.axis_size("case")
    per = pressure.shape[0] // groups
    total = layers * slabs
    spreads = exchange_halo(panel, flags, diagonal, slabs)
    wide = [x.reshape((-1,) + panel.shape[1:]) for x in spreads]
    fields, gram, cross = solve(pressure, *wide, total, layers, radial, around, per)
    scale = 1.0 / (total * radial * around)
    return (fields, gram * scale, cross * scale)


def solution(mesh):
    in_specs = (P(), P("slab", None, None), P("slab", None, None), P("slab", None, None))
    out_specs = (P("case", "slab", None, None), P("case", None), P("case", None))
    return jax.shard_map(local, mesh=mesh, in_specs=in_specs, out_specs=out_specs, check_vma=False)
```
